128 devices in a mesh: chord: 4 (over x_lo, core), normal: 32 (over x_hi, y, z).
Axes of the slice: x: 4 (x_hi: 2, x_lo: 2; x = x_hi * 2 + x_lo), y: 4, z: 4, core: 2. Of those that a mesh axis runs over, the one named last changes fastest.
Arguments:
- direct_modes: bfloat16 [16, 5, 64, 512, 256], P(None, None, 'chord', 'normal'), may hold values from -62 to 62
- adjoint_modes: bfloat16 [16, 5, 64, 512, 256], P(None, None, 'chord', 'normal'), may hold values from -5 to 5
- base_flow: float32 [5, 64, 512, 256], P(None, 'chord', 'normal'), may hold values from -5 to 5
- cell_type: int32 [64, 512, 256], P('chord', 'normal'), may hold values from 0 to 2
- mode_pick: int32 [16], replicated, may hold values from 0 to 15, each once
- flux_mix: float32 [3, 5, 5], replicated, may hold values from -2.5 to 2.5
Outputs:
- sensitivity: float32 [5, 64, 512, 256], P(None, 'chord', 'normal')
The draws below stay inside these ranges and needn't reach their ends.
Inputs may be any that keep to these rules, and one draw needn't show every extreme that they name: `mode_pick`: each mode once.
All inputs are finite; a program needn't handle non-finite values.
Results may differ from the reference program's by a relative error of at most 0.0003.
Values may be sent and summed in bfloat16 or wider, within the bound.
A program may use at most 256 MiB of HBM per device.

```python
import math
import jax
import jax.numpy as jnp
from jax import lax

M = 16
VARS = 5
NX = 64
NY = 512
NZ = 256


def draw_direct_modes(key, part):
    key_one = jax.random.fold_in(key, 0)
    shape = (M, VARS, NX, NY, NZ)
    rows = jnp.arange(NY, dtype=jnp.float32).reshape(1, 1, 1, NY, 1)
    rising = jnp.exp(math.log(3.0) * rows / max(NY - 1, 1))
    values = jnp.clip(jax.random.normal(key_one, shape, jnp.float32), -4.0, 4.0)
    result = values * rising
    return result.astype(jnp.bfloat16)


def set_ends(entries, own_key, low, top_value):
    shape = entries.shape
    place = [jax.random.randint(jax.random.fold_in(own_key, axis), (), 0, shape[axis]) for axis in range(len(shape))]
    entries = entries.at[tuple(place)].set(low)
    longest = shape.index(max(shape))
    place[longest] = (place[longest] + 1) % shape[longest]
    return entries.at[tuple(place)].set(top_value)


def block_levels(stream_key, dims, cuts, least, high):
    loudness, own = 1.0, jax.random.fold_in(stream_key, 6)
    for dim, parts in cuts:
        steps = jnp.exp(jax.random.uniform(jax.random.fold_in(own, dim), (parts,), jnp.float32, least / len(cuts), high / len(cuts)))
        loudness = loudness * jnp.repeat(steps, dims[dim] // parts).reshape([-1 if axis == dim else 1 for axis in range(len(dims))])
    return loudness


def noise(own_key, shape, width, reach, cuts=(), kind=jnp.bfloat16):
    level = block_levels(own_key, shape, cuts, -0.22, 0.18) if cuts else 1.0
    values = jax.random.normal(own_key, shape, jnp.float32) * width * level
    return jnp.minimum(jnp.maximum(values, -reach), reach).astype(kind)


def setup_inputs(seed: int = 0) -> dict:
    streams_of = jax.random.split(jax.random.key(seed), 7)
    direct_modes = draw_direct_modes(jax.random.fold_in(streams_of[6], 71), 0)
    adjoint_modes = noise(streams_of[1], (M, VARS, NX, NY, NZ), 1.0, 5.0, ((2, 4), (3, 32)))
    base_flow = noise(streams_of[2], (VARS, NX, NY, NZ), 0.7, 5.0, ((1, 4), (2, 32)), jnp.float32)
    cell_type = set_ends(jax.random.randint(streams_of[3], (NX, NY, NZ), 0, 3), jax.random.fold_in(streams_of[3], 1), 0, 2).astype(jnp.int32)
    mode_pick = jax.random.permutation(streams_of[4], M).astype(jnp.int32)
    flux_mix = noise(streams_of[5], (3, VARS, VARS), VARS ** -0.5, 2.5, (), jnp.float32)
    return dict(direct_modes=direct_modes, adjoint_modes=adjoint_modes, base_flow=base_flow, cell_type=cell_type, mode_pick=mode_pick, flux_mix=flux_mix)


def mixing(matrix, field_in):
    return jnp.einsum('ij,i...->j...', matrix, field_in, precision=lax.Precision.HIGHEST)

def diff_chord(padded):
    return padded[..., 2:, 1:-1, :] - padded[..., :-2, 1:-1, :]

def diff_normal(padded):
    return padded[..., 1:-1, 2:, :] - padded[..., 1:-1, :-2, :]

def inner_cells(padded):
    return padded[..., 1:-1, 1:-1, :]

def diff_span(field_in):
    return jnp.roll(field_in, -1, -1) - jnp.roll(field_in, 1, -1)

def pad_plane(field_in):
    return jnp.pad(field_in, [(0, 0)] * (field_in.ndim - 3) + [(1, 1), (1, 1), (0, 0)])

def bilinear_term(left_pad, right_pad, flux_mix):
    summed = jnp.zeros(inner_cells(left_pad).shape, jnp.float32)
    for axis_num, differ in ((0, diff_chord), (1, diff_normal)):
        mixed_adj = mixing(flux_mix[axis_num], right_pad)
        summed = summed + differ(left_pad) * inner_cells(mixed_adj) - differ(left_pad * mixed_adj)
    left_in = inner_cells(left_pad)
    mixed_adj = mixing(flux_mix[2], inner_cells(right_pad))
    return summed + diff_span(left_in) * mixed_adj - diff_span(left_in * mixed_adj)

def cell_weight(cell_type):
    return jnp.where(cell_type == 0, 1.0, jnp.where(cell_type == 1, 0.5, 0.0)).astype(jnp.float32)

def reference(direct_modes, adjoint_modes, base_flow, cell_type, mode_pick, flux_mix):
    modes_count = direct_modes.shape[0]
    energy = lax.map(lambda single: jnp.mean(jnp.square(single.astype(jnp.float32))), direct_modes)
    amplitude = lax.rsqrt(energy + 1e-06)

    def accumulate(summed, number):
        direct = pad_plane(direct_modes[number].astype(jnp.float32))
        adjoint = pad_plane(adjoint_modes[mode_pick[number]].astype(jnp.float32))
        return (summed + amplitude[number] * bilinear_term(direct, adjoint, flux_mix), None)
    gradient, _ = lax.scan(accumulate, jnp.zeros(base_flow.shape, jnp.float32), jnp.arange(modes_count, dtype=jnp.int32))
    gradient = gradient / modes_count
    weight = cell_weight(cell_type)
    base_pad = pad_plane(base_flow)
    once_applied = bilinear_term(base_pad, pad_plane(weight * gradient), flux_mix)
    return bilinear_term(base_pad, pad_plane(weight * once_applied), flux_mix)
```

```python
import functools

import jax
import jax.numpy as jnp
from jax import lax
from jax.experimental import pallas as pl
from jax.experimental.pallas import tpu as pltpu
from jax.sharding import PartitionSpec as P

MESH = pl.DeviceIdType.MESH
F32 = jnp.float32
BF16 = jnp.bfloat16
GROUP = 4


def iota(shape, dim):
    return lax.broadcasted_iota(jnp.int32, shape, dim)


def diff_lanes(x):
    lanes = x.shape[-1]
    return pltpu.roll(x, lanes - 1, 1) - pltpu.roll(x, 1, 1)


def rows_up(x):
    rows = x.shape[0]
    return jnp.where(iota(x.shape, 0) == rows - 1, 0.0, pltpu.roll(x, rows - 1, 0))


def rows_down(x):
    return jnp.where(iota(x.shape, 0) == 0, 0.0, pltpu.roll(x, 1, 0))


def split3(x):
    high = x.astype(BF16)
    low = (x - high.astype(F32)).astype(BF16)
    return jnp.concatenate([high, low, high], axis=0)


def dot(a, b):
    return jnp.dot(a, b, preferred_element_type=F32)


def kernel(
    sizes,
    u_hbm, v_hbm, base_hbm, cell_hbm, pick, mix,
    out_hbm,
    u, v, base, cell, uface, vface, uhalo, wface, mats, mat2, mat0, select, circ,
    w_scr, du_scr, acc, grad, sx, sface, shalo, ysend, yhalo, field, wall, base_dz, bface, bhalo,
    fterm, energy, round_one, round_two, round_three, amp, weight, result,
    load_sem, usend_sem, urecv_sem, xs_sem, xr_sem, ys_sem, yr_sem, es_sem, er_sem, out_sem,
):
    nc, nn, modes, nv, nx, ny, nz = sizes
    kv = nv * ny
    c, n = lax.axis_index("chord"), lax.axis_index("normal")
    has_x = (c > 0, c < nc - 1)
    has_y = (n > 0, n < nn - 1)
    step = (-1, 1)
    zs, rest = 4, nn // 4
    groups = modes // GROUP

    def u_load(g):
        s = pl.ds(g * GROUP, GROUP)
        return pltpu.make_async_copy(u_hbm.at[s], u.at[s, :, pl.ds(1, nx)], load_sem.at[g])

    def v_load(g):
        s = pl.ds(g * GROUP, GROUP)
        return pltpu.make_async_copy(v_hbm.at[s], v.at[s], load_sem.at[groups + g])

    base_load = pltpu.make_async_copy(base_hbm, base.at[:, pl.ds(1, nx)], load_sem.at[2 * groups])
    cell_load = pltpu.make_async_copy(cell_hbm, cell, load_sem.at[2 * groups + 1])
    for g in range(groups):
        u_load(g).start()
    base_load.start()
    cell_load.start()
    for g in range(groups):
        v_load(g).start()

    first = [(lax.rem(c + k, nc), n) for k in range(1, nc)]
    second = [(c, n // zs * zs + lax.rem(lax.rem(n, zs) + k, zs)) for k in range(1, zs)]
    third = [(c, lax.rem(n // zs + k, rest) * zs + lax.rem(n, zs)) for k in range(1, rest)]
    around = [(c, lax.rem(n + 1, nn)), (c, lax.rem(n + nn - 1, nn))]
    barrier = pltpu.get_barrier_semaphore()
    peers = first + second + third + around
    for peer in peers:
        pl.semaphore_signal(barrier, inc=1, device_id=peer, device_id_type=MESH)

    @pl.when(c == 0)
    def _():
        u[:, :, 0] = jnp.zeros((modes, nv, ny, nz), BF16)
        base[:, 0] = jnp.zeros((nv, ny, nz), F32)
        sx[:, 0] = jnp.zeros((nv, ny, nz), F32)
        field[0, :, 0] = jnp.zeros((nv, ny, nz), F32)
        field[1, :, 0] = jnp.zeros((nv, ny, nz), F32)

    @pl.when(c == nc - 1)
    def _():
        u[:, :, nx + 1] = jnp.zeros((modes, nv, ny, nz), BF16)
        base[:, nx + 1] = jnp.zeros((nv, ny, nz), F32)
        sx[:, nx + 1] = jnp.zeros((nv, ny, nz), F32)
        field[0, :, nx + 1] = jnp.zeros((nv, ny, nz), F32)
        field[1, :, nx + 1] = jnp.zeros((nv, ny, nz), F32)

    for side, at_edge in ((0, n == 0), (1, n == nn - 1)):
        @pl.when(at_edge)
        def _():
            uhalo[side] = jnp.zeros((modes, nv, nx, nz), BF16)
            bhalo[side] = jnp.zeros((nv, nx, nz), F32)
            shalo[side] = jnp.zeros((nv, nx, nz), F32)
            yhalo[0, side] = jnp.zeros((nv, nx, nz), F32)
            yhalo[1, side] = jnp.zeros((nv, nx, nz), F32)

    pl.semaphore_wait(barrier, len(peers))

    def x_copy(kind, way, src, dst):
        return pltpu.make_async_remote_copy(
            src_ref=src, dst_ref=dst, send_sem=xs_sem.at[kind, way], recv_sem=xr_sem.at[kind, 1 - way],
            device_id=(lax.rem(c + step[way] + nc, nc), n), device_id_type=MESH)

    def y_copy(send_sems, recv_sems, kind, way, src, dst):
        return pltpu.make_async_remote_copy(
            src_ref=src, dst_ref=dst, send_sem=send_sems.at[kind, way], recv_sem=recv_sems.at[kind, 1 - way],
            device_id=(c, lax.rem(n + step[way] + nn, nn)), device_id_type=MESH)

    x_links = [
        lambda w: x_copy(0, w, u_hbm.at[:, :, (nx - 1) * w], u.at[:, :, (nx + 1) * (1 - w)]),
        lambda w: x_copy(1, w, base_hbm.at[:, (nx - 1) * w], base.at[:, (nx + 1) * (1 - w)]),
        lambda w: x_copy(2, w, sx.at[:, 1 + (nx - 1) * w], sx.at[:, (nx + 1) * (1 - w)]),
        lambda w: x_copy(3, w, field.at[0, :, 1 + (nx - 1) * w], field.at[0, :, (nx + 1) * (1 - w)]),
        lambda w: x_copy(4, w, field.at[1, :, 1 + (nx - 1) * w], field.at[1, :, (nx + 1) * (1 - w)]),
    ]
    y_links = [
        lambda w: y_copy(ys_sem, yr_sem, 0, w, bface.at[w], bhalo.at[1 - w]),
        lambda w: y_copy(ys_sem, yr_sem, 1, w, sface.at[w], shalo.at[1 - w]),
        lambda w: y_copy(ys_sem, yr_sem, 2, w, ysend.at[0, w], yhalo.at[0, 1 - w]),
        lambda w: y_copy(ys_sem, yr_sem, 3, w, ysend.at[1, w], yhalo.at[1, 1 - w]),
    ]

    def u_link(g):
        s = pl.ds(g * GROUP, GROUP)
        return lambda w: y_copy(usend_sem, urecv_sem, g, w, uface.at[w, s], uhalo.at[1 - w, s])

    def send(link, has):
        for w in (0, 1):
            @pl.when(has[w])
            def _():
                link(w).start()

    def receive(link, has):
        for side in (0, 1):
            @pl.when(has[side])
            def _():
                link(1 - side).wait_recv()

    def drain(link, has):
        for w in (0, 1):
            @pl.when(has[w])
            def _():
                link(w).wait_send()

    send(x_links[0], has_x)
    send(x_links[1], has_x)

    pick_row = iota((2 * nx, nx * ny), 0)
    from_row = iota((2 * nx, nx * ny), 1)
    wanted = jnp.where(pick_row < nx, pick_row * ny, (pick_row - nx) * ny + ny - 1)
    select[...] = jnp.where(from_row == wanted, 1.0, 0.0).astype(BF16)
    lane_in, lane_out = iota((nz, nz), 0), iota((nz, nz), 1)
    ahead = jnp.where(lane_out == nz - 1, 0, lane_out + 1)
    behind = jnp.where(lane_out == 0, nz - 1, lane_out - 1)
    circ[...] = (jnp.where(lane_in == ahead, 1.0, 0.0) - jnp.where(lane_in == behind, 1.0, 0.0)).astype(BF16)

    def faces_of(block, faces, m):
        for i in range(nv):
            both = dot(select[...], block(m, i).reshape(nx * ny, nz))
            faces[0, m, i] = both[:nx].astype(BF16)
            faces[1, m, i] = both[nx:].astype(BF16)

    for g in range(groups):
        u_load(g).wait()

        def u_mode(m, carry):
            total = jnp.zeros((ny, nz), F32)
            for i in range(nv):
                for x in range(nx):
                    cells = u[m, i, 1 + x].astype(F32)
                    total = total + cells * cells
            total = jnp.sum(total, axis=0, keepdims=True)
            energy[pl.ds(m, 1), :] = total[:, :128] + total[:, 128:]
            faces_of(lambda m, i: u[m, i, pl.ds(1, nx)], uface, m)
            return carry

        lax.fori_loop(g * GROUP, (g + 1) * GROUP, u_mode, 0)
        send(u_link(g), has_y)

    def e_copy(index, peer, dst):
        return pltpu.make_async_remote_copy(
            src_ref=energy.at[pl.ds(modes * (0 if index < nc - 1 else 1 if index < nc + zs - 2 else 2), modes)],
            dst_ref=dst, send_sem=es_sem.at[index], recv_sem=er_sem.at[index], device_id=peer, device_id_type=MESH)

    ones = [e_copy(k, first[k], round_one.at[k]) for k in range(nc - 1)]
    twos = [e_copy(nc - 1 + k, second[k], round_two.at[k]) for k in range(zs - 1)]
    threes = [e_copy(nc + zs - 2 + k, third[k], round_three.at[k]) for k in range(rest - 1)]

    def v_faces(g):
        v_load(g).wait()

        def v_mode(m, carry):
            faces_of(lambda m, i: v[m, i], vface, m)
            return carry

        lax.fori_loop(g * GROUP, (g + 1) * GROUP, v_mode, 0)

    def finish(copies, slots, src):
        total = energy[pl.ds(modes * src, modes), :]
        for k, copy in enumerate(copies):
            copy.wait_recv()
            total = total + slots[k]
        return total

    for copy in ones:
        copy.start()
    v_faces(0)
    energy[pl.ds(modes, modes), :] = finish(ones, round_one, 0)
    for copy in twos:
        copy.start()

    width = 3 * kv
    lane = iota((ny, width), 1)
    row = iota((ny, width), 0)
    lane_row = lax.rem(lane, ny)
    lane_var = lax.rem(lane, kv) // ny
    same = jnp.where(lane_row == row, 1.0, 0.0)
    nxt = jnp.where(lane_row == row + 1, 1.0, 0.0)
    prv = jnp.where(lane_row == row - 1, 1.0, 0.0)
    kinds = ((0, same), (1, nxt - same), (1, same - prv), (2, same), (1, same))
    for k, (d, stencil) in enumerate(kinds):
        for j in range(nv):
            coefs = jnp.zeros((ny, width), F32)
            for i in range(nv):
                coefs = jnp.where(lane_var == i, mix[d, i, j], coefs)
            mat0[pl.ds((k * nv + j) * ny, ny), :] = coefs * stencil
    high = mat0[...].astype(BF16)
    low = (mat0[...] - high.astype(F32)).astype(BF16)
    mat2[...] = jnp.where(iota(mat0.shape, 1) < 2 * kv, high.astype(F32), low.astype(F32)).astype(BF16)

    v_faces(1)
    energy[pl.ds(2 * modes, modes), :] = finish(twos, round_two, 1)
    for copy in threes:
        copy.start()
    v_faces(2)

    cell_load.wait()
    base_load.wait()
    kind_of = cell[...]
    weight[...] = jnp.where(kind_of == 0, 1.0, jnp.where(kind_of == 1, 0.5, 0.0)).astype(F32)
    for side in (0, 1):
        for x in range(nx):
            bface[side, :, pl.ds(x, 1), :] = base[:, 1 + x, pl.ds((ny - 1) * side, 1), :]
    send(y_links[0], has_y)

    def base_plane(x, carry):
        for j in range(nv):
            base_dz[j, x] = diff_lanes(base[j, 1 + x])
        return carry

    lax.fori_loop(0, nx, base_plane, 0)
    v_faces(3)

    cells_all = nc * nn * nv * nx * ny * nz
    total = jnp.sum(finish(threes, round_three, 2), axis=1, keepdims=True)
    amp[...] = jnp.broadcast_to(lax.rsqrt(total / cells_all + 1e-06) / modes, amp.shape)

    def mode_matrix(m, carry):
        scaled = mat0[:, pl.ds(0, 2 * kv)] * amp[pl.ds(m, 1), pl.ds(0, 2 * kv)]
        big = scaled.astype(BF16).astype(F32)
        mats[m] = jnp.where(iota(scaled.shape, 1) < kv, big, scaled - big).astype(BF16)
        return carry

    lax.fori_loop(0, modes, mode_matrix, 0)

    sface[...] = jnp.zeros(sface.shape, F32)
    sx[:, 1] = jnp.zeros((nv, ny, nz), F32)
    sx[:, nx] = jnp.zeros((nv, ny, nz), F32)

    def face_mode(m, carry):
        p = pick[m]
        for s in (0, 1):
            rows = vface[s, p].reshape(kv, nz)
            w = dot(mats[m, pl.ds(4 * kv, kv), :], jnp.concatenate([rows, rows], axis=0))
            wface[s, m] = w
            sface[s] += w.reshape(nv, nx, nz) * uface[s, m].astype(F32)
            rows = v[p, :, (nx - 1) * s].reshape(kv, nz)
            w = dot(mats[m, pl.ds(0, kv), :], jnp.concatenate([rows, rows], axis=0))
            x = 1 + (nx - 1) * s
            sx[:, x] += w.reshape(nv, ny, nz) * u[m, :, x].astype(F32)
        return carry

    lax.fori_loop(0, modes, face_mode, 0)
    send(x_links[2], has_x)
    send(y_links[1], has_y)

    def plane(x):
        def group(g, carry):
            m0 = g * GROUP
            du_scr[...] = dot(u[pl.ds(m0, GROUP), :, x].reshape(GROUP * kv, nz), circ[...])
            for k in range(GROUP):
                rows = v[pick[m0 + k], :, x - 1].reshape(kv, nz)
                w_scr[k] = dot(mats[m0 + k, pl.ds(0, 4 * kv), :], jnp.concatenate([rows, rows], axis=0))
            for j in range(nv):
                q, s_x, s_z, up, down = (acc[t, j] for t in range(5))
                for k in range(GROUP):
                    here = u[m0 + k, j, x].astype(F32)
                    dx = u[m0 + k, j, x + 1].astype(F32) - u[m0 + k, j, x - 1].astype(F32)
                    dz = du_scr[pl.ds(k * kv + j * ny, ny), :]
                    wx, wp, wm, wz = (w_scr[k, pl.ds(t * kv + j * ny, ny), :] for t in range(4))
                    q = q + dx * wx + dz * wz
                    s_x = s_x + here * wx
                    s_z = s_z + here * wz
                    up = up + here * wm
                    down = down + here * wp
                for t, value in enumerate((q, s_x, s_z, up, down)):
                    acc[t, j] = value
            return carry

        acc[...] = jnp.zeros(acc.shape, F32)
        lax.fori_loop(0, groups, group, 0)
        for j in range(nv):
            grad[j, x - 1] = acc[0, j] - diff_lanes(acc[2, j]) - rows_up(acc[3, j]) - rows_down(acc[4, j])

    def inner_plane(x, carry):
        plane(x)
        for j in range(nv):
            sx[j, x] = acc[1, j]
        return carry

    lax.fori_loop(2, nx, inner_plane, 0)
    receive(x_links[0], has_x)

    def end_plane(s, carry):
        plane(1 + (nx - 1) * s)
        return carry

    lax.fori_loop(0, 2, end_plane, 0)

    for g in range(groups):
        receive(u_link(g), has_y)
    fterm[...] = jnp.zeros(fterm.shape, F32)

    def cross_mode(m, carry):
        for s in (0, 1):
            fterm[s] += wface[s, m].reshape(nv, nx, nz) * uhalo[s, m].astype(F32)
        return carry

    lax.fori_loop(0, modes, cross_mode, 0)
    receive(y_links[1], has_y)
    receive(x_links[2], has_x)
    fterm[0] = shalo[0] - fterm[0]
    fterm[1] = fterm[1] - shalo[1]

    def add_rows(target, x0):
        for side in (0, 1):
            for x in range(nx):
                end = pl.ds((ny - 1) * side, 1)
                target[:, x + x0, end, :] = target[:, x + x0, end, :] + fterm[side, :, pl.ds(x, 1), :]

    def grad_plane(x, carry):
        for j in range(nv):
            grad[j, x] = grad[j, x] - (sx[j, x + 2] - sx[j, x])
        return carry

    lax.fori_loop(0, nx, grad_plane, 0)
    add_rows(grad, 0)

    def apply(slot, source, target):
        def weigh(x, carry):
            for j in range(nv):
                field[slot, j, x + 1] = weight[x] * source[j, x]
            return carry

        lax.fori_loop(0, nx, weigh, 0)
        for side in (0, 1):
            for x in range(nx):
                ysend[slot, side, :, pl.ds(x, 1), :] = field[slot, :, 1 + x, pl.ds((ny - 1) * side, 1), :]
        send(x_links[3 + slot], has_x)
        send(y_links[2 + slot], has_y)

        def mixed(x, carry):
            wall[x] = dot(mat2[pl.ds(0, 4 * kv), :], split3(field[slot, :, x].reshape(kv, nz)))
            return carry

        lax.fori_loop(1, nx + 1, mixed, 0)
        own = [dot(mat2[pl.ds(4 * kv, kv), :], split3(ysend[slot, s].reshape(kv, nz))) for s in (0, 1)]
        for s in (0, 1):
            wface[s, 0] = own[s]

        def result_plane(x, carry):
            for j in range(nv):
                r = pl.ds(j * ny, ny)
                wx = wall[x, r, :]
                wp, wm, wz = (wall[x, pl.ds(t * kv + j * ny, ny), :] for t in (1, 2, 3))
                here = base[j, x]
                value = base[j, x + 1] * (wx - wall[x + 1, r, :]) - base[j, x - 1] * (wx - wall[x - 1, r, :])
                value = value + base_dz[j, x - 1] * wz - diff_lanes(here * wz)
                target[j, x - 1] = value - rows_up(here * wm) - rows_down(here * wp)
            return carry

        lax.fori_loop(2, nx, result_plane, 0)
        if slot == 0:
            receive(x_links[1], has_x)
            receive(y_links[0], has_y)
        receive(x_links[3 + slot], has_x)
        receive(y_links[2 + slot], has_y)
        for x in (0, nx + 1):
            wall[x, pl.ds(0, kv), :] = dot(mat2[pl.ds(0, kv), :], split3(field[slot, :, x].reshape(kv, nz)))
        lax.fori_loop(0, 2, lambda s, carry: result_plane(1 + (nx - 1) * s, carry), 0)
        for s in (0, 1):
            far = dot(mat2[pl.ds(4 * kv, kv), :], split3(yhalo[slot, s].reshape(kv, nz)))
            change = (far - wface[s, 0]).reshape(nv, nx, nz) * bhalo[s]
            fterm[s] = change if s == 0 else -change
        add_rows(target, 0)

    apply(0, grad, result)
    apply(1, result, grad)
    store = pltpu.make_async_copy(grad, out_hbm, out_sem)
    store.start()
    for g in range(groups):
        drain(u_link(g), has_y)
    for link in x_links:
        drain(link, has_x)
    for link in y_links:
        drain(link, has_y)
    for copy in ones + twos + threes:
        copy.wait_send()
    store.wait()


def per_device(u, v, base, cell, pick, mix, *, interpret=False):
    modes, nv, nx, ny, nz = u.shape
    nc, nn = lax.axis_size("chord"), lax.axis_size("normal")
    kv = nv * ny
    groups = modes // GROUP
    vm = pltpu.VMEM
    any_space = pl.BlockSpec(memory_space=pl.ANY)
    smem = pl.BlockSpec(memory_space=pltpu.SMEM)
    return pl.pallas_call(
        functools.partial(kernel, (nc, nn, modes, nv, nx, ny, nz)),
        out_shape=jax.ShapeDtypeStruct(base.shape, F32),
        in_specs=[any_space] * 4 + [smem] * 2,
        out_specs=any_space,
        scratch_shapes=[
            vm((modes, nv, nx + 2, ny, nz), BF16),
            vm((modes, nv, nx, ny, nz), BF16),
            vm((nv, nx + 2, ny, nz), F32),
            vm((nx, ny, nz), jnp.int32),
            vm((2, modes, nv, nx, nz), BF16),
            vm((2, modes, nv, nx, nz), BF16),
            vm((2, modes, nv, nx, nz), BF16),
            vm((2, modes, kv, nz), F32),
            vm((modes, 5 * kv, 2 * kv), BF16),
            vm((5 * kv, 3 * kv), BF16),
            vm((5 * kv, 3 * kv), F32),
            vm((2 * nx, nx * ny), BF16),
            vm((nz, nz), BF16),
            vm((GROUP, 4 * kv, nz), F32),
            vm((GROUP * kv, nz), F32),
            vm((5, nv, ny, nz), F32),
            vm((nv, nx, ny, nz), F32),
            vm((nv, nx + 2, ny, nz), F32),
            vm((2, nv, nx, nz), F32),
            vm((2, nv, nx, nz), F32),
            vm((2, 2, nv, nx, nz), F32),
            vm((2, 2, nv, nx, nz), F32),
            vm((2, nv, nx + 2, ny, nz), F32),
            vm((nx + 2, 4 * kv, nz), F32),
            vm((nv, nx, ny, nz), F32),
            vm((2, nv, nx, nz), F32),
            vm((2, nv, nx, nz), F32),
            vm((2, nv, nx, nz), F32),
            vm((3 * modes, 128), F32),
            vm((nc - 1, modes, 128), F32),
            vm((3, modes, 128), F32),
            vm((max(nn // 4 - 1, 1), modes, 128), F32),
            vm((modes, 256), F32),
            vm((nx, ny, nz), F32),
            vm((nv, nx, ny, nz), F32),
            pltpu.SemaphoreType.DMA((2 * groups + 2,)),
            pltpu.SemaphoreType.DMA((groups, 2)),
            pltpu.SemaphoreType.DMA((groups, 2)),
            pltpu.SemaphoreType.DMA((5, 2)),
            pltpu.SemaphoreType.DMA((5, 2)),
            pltpu.SemaphoreType.DMA((4, 2)),
            pltpu.SemaphoreType.DMA((4, 2)),
            pltpu.SemaphoreType.DMA((nc + nn // 4 + 1,)),
            pltpu.SemaphoreType.DMA((nc + nn // 4 + 1,)),
            pltpu.SemaphoreType.DMA,
        ],
        compiler_params=pltpu.CompilerParams(
            collective_id=0, has_side_effects=True, vmem_limit_bytes=60 * 2**20),
    )(u, v, base, cell, pick, mix)


def solution(mesh):
    return jax.shard_map(
        per_device,
        mesh=mesh,
        in_specs=(
            P(None, None, "chord", "normal", None),
            P(None, None, "chord", "normal", None),
            P(None, "chord", "normal", None),
            P("chord", "normal", None),
            P(),
            P(),
        ),
        out_specs=P(None, "chord", "normal", None),
        check_vma=False,
    )
```

```python
import functools

import jax
import jax.numpy as jnp
from jax import lax
from jax.experimental import pallas as pl
from jax.experimental.pallas import tpu as pltpu
from jax.sharding import PartitionSpec as P

MESH = pl.DeviceIdType.MESH
F32 = jnp.float32
BF16 = jnp.bfloat16
GROUP = 4


def iota(shape, dim):
    return lax.broadcasted_iota(jnp.int32, shape, dim)


def diff_lanes(x):
    lanes = x.shape[-1]
    return pltpu.roll(x, lanes - 1, 1) - pltpu.roll(x, 1, 1)


def rows_up(x):
    rows = x.shape[0]
    return jnp.where(iota(x.shape, 0) == rows - 1, 0.0, pltpu.roll(x, rows - 1, 0))


def rows_down(x):
    return jnp.where(iota(x.shape, 0) == 0, 0.0, pltpu.roll(x, 1, 0))


def split3(x):
    high = x.astype(BF16)
    low = (x - high.astype(F32)).astype(BF16)
    return jnp.concatenate([high, low, high], axis=0)


def dot(a, b):
    return jnp.dot(a, b, preferred_element_type=F32)


def kernel(
    sizes,
    u_hbm, v_hbm, base_hbm, cell_hbm, pick, mix,
    out_hbm,
    u, v, base, cell, uface, vface, uhalo, wface, mats, mat2, mat0, select, circ,
    w_scr, du_scr, acc, grad, sx, sx_all, sface, shalo, ysend, yhalo, field, wall, base_dz, bface, bhalo,
    fterm, energy, round_one, round_two, round_three, amp, weight, result,
    load_sem, xs_sem, xr_sem, ys_sem, yr_sem, es_sem, er_sem, out_sem,
):
    nc, nn, modes, nv, nx, ny, nz = sizes
    kv = nv * ny
    c, n = lax.axis_index("chord"), lax.axis_index("normal")
    has_x = (c > 0, c < nc - 1)
    has_y = (n > 0, n < nn - 1)
    step = (-1, 1)
    zs, rest = 4, nn // 4
    groups = modes // GROUP

    def u_load(g):
        s = pl.ds(g * GROUP, GROUP)
        return pltpu.make_async_copy(u_hbm.at[s], u.at[s, :, pl.ds(1, nx)], load_sem.at[g])

    def v_load(g):
        s = pl.ds(g * GROUP, GROUP)
        return pltpu.make_async_copy(v_hbm.at[s], v.at[s], load_sem.at[groups + g])

    base_load = pltpu.make_async_copy(base_hbm, base.at[:, pl.ds(1, nx)], load_sem.at[2 * groups])
    cell_load = pltpu.make_async_copy(cell_hbm, cell, load_sem.at[2 * groups + 1])
    for g in range(groups):
        u_load(g).start()
    base_load.start()
    cell_load.start()
    for g in range(groups):
        v_load(g).start()

    first = [(lax.rem(c + k, nc), n) for k in range(1, nc)]
    second = [(c, n // zs * zs + lax.rem(lax.rem(n, zs) + k, zs)) for k in range(1, zs)]
    third = [(c, lax.rem(n // zs + k, rest) * zs + lax.rem(n, zs)) for k in range(1, rest)]
    around = [(c, lax.rem(n + 1, nn)), (c, lax.rem(n + nn - 1, nn))]
    barrier = pltpu.get_barrier_semaphore()
    peers = first + second + third + around
    for peer in peers:
        pl.semaphore_signal(barrier, inc=1, device_id=peer, device_id_type=MESH)

    @pl.when(c == 0)
    def _():
        u[:, :, 0] = jnp.zeros((modes, nv, ny, nz), BF16)
        base[:, 0] = jnp.zeros((nv, ny, nz), F32)
        sx[:, 0] = jnp.zeros((nv, ny, nz), F32)
        field[0, :, 0] = jnp.zeros((nv, ny, nz), F32)
        field[1, :, 0] = jnp.zeros((nv, ny, nz), F32)

    @pl.when(c == nc - 1)
    def _():
        u[:, :, nx + 1] = jnp.zeros((modes, nv, ny, nz), BF16)
        base[:, nx + 1] = jnp.zeros((nv, ny, nz), F32)
        sx[:, 3] = jnp.zeros((nv, ny, nz), F32)
        field[0, :, nx + 1] = jnp.zeros((nv, ny, nz), F32)
        field[1, :, nx + 1] = jnp.zeros((nv, ny, nz), F32)

    for side, at_edge in ((0, n == 0), (1, n == nn - 1)):
        @pl.when(at_edge)
        def _():
            uhalo[side] = jnp.zeros((modes, nv, nx, nz), BF16)
            bhalo[side] = jnp.zeros((nv, nx, nz), F32)
            shalo[side] = jnp.zeros((nv, nx, nz), F32)
            yhalo[0, side] = jnp.zeros((nv, nx, nz), F32)
            yhalo[1, side] = jnp.zeros((nv, nx, nz), F32)

    pl.semaphore_wait(barrier, len(peers))

    def x_copy(kind, way, src, dst):
        return pltpu.make_async_remote_copy(
            src_ref=src, dst_ref=dst, send_sem=xs_sem.at[kind, way], recv_sem=xr_sem.at[kind, 1 - way],
            device_id=(lax.rem(c + step[way] + nc, nc), n), device_id_type=MESH)

    def y_copy(kind, way, src, dst):
        return pltpu.make_async_remote_copy(
            src_ref=src, dst_ref=dst, send_sem=ys_sem.at[kind, way], recv_sem=yr_sem.at[kind, 1 - way],
            device_id=(c, lax.rem(n + step[way] + nn, nn)), device_id_type=MESH)

    x_links = [
        lambda w: x_copy(0, w, u_hbm.at[:, :, (nx - 1) * w], u.at[:, :, (nx + 1) * (1 - w)]),
        lambda w: x_copy(1, w, base_hbm.at[:, (nx - 1) * w], base.at[:, (nx + 1) * (1 - w)]),
        lambda w: x_copy(2, w, sx.at[:, 1 + w], sx.at[:, 3 * (1 - w)]),
        lambda w: x_copy(3, w, field.at[0, :, 1 + (nx - 1) * w], field.at[0, :, (nx + 1) * (1 - w)]),
        lambda w: x_copy(4, w, field.at[1, :, 1 + (nx - 1) * w], field.at[1, :, (nx + 1) * (1 - w)]),
    ]
    y_links = [
        lambda w: y_copy(0, w, bface.at[w], bhalo.at[1 - w]),
        lambda w: y_copy(1, w, sface.at[w], shalo.at[1 - w]),
        lambda w: y_copy(2, w, ysend.at[0, w], yhalo.at[0, 1 - w]),
        lambda w: y_copy(3, w, ysend.at[1, w], yhalo.at[1, 1 - w]),
        lambda w: y_copy(4, w, uface.at[w], uhalo.at[1 - w]),
    ]

    def send(link, has):
        for w in (0, 1):
            @pl.when(has[w])
            def _():
                link(w).start()

    def receive(link, has):
        for side in (0, 1):
            @pl.when(has[side])
            def _():
                link(1 - side).wait_recv()

    def drain(link, has):
        for w in (0, 1):
            @pl.when(has[w])
            def _():
                link(w).wait_send()

    pick_row = iota((2 * nx, nx * ny), 0)
    from_row = iota((2 * nx, nx * ny), 1)
    wanted = jnp.where(pick_row < nx, pick_row * ny, (pick_row - nx) * ny + ny - 1)
    select[...] = jnp.where(from_row == wanted, 1.0, 0.0).astype(BF16)
    lane_in, lane_out = iota((nz, nz), 0), iota((nz, nz), 1)
    ahead = jnp.where(lane_out == nz - 1, 0, lane_out + 1)
    behind = jnp.where(lane_out == 0, nz - 1, lane_out - 1)
    circ[...] = (jnp.where(lane_in == ahead, 1.0, 0.0) - jnp.where(lane_in == behind, 1.0, 0.0)).astype(BF16)

    def faces_of(block, faces, m):
        for i in range(nv):
            both = dot(select[...], block(m, i).reshape(nx * ny, nz))
            faces[0, m, i] = both[:nx].astype(BF16)
            faces[1, m, i] = both[nx:].astype(BF16)

    for g in range(groups):
        u_load(g).wait()

        def u_mode(m, carry):
            total = jnp.zeros((ny, nz), F32)
            for i in range(nv):
                for x in range(nx):
                    cells = u[m, i, 1 + x].astype(F32)
                    total = total + cells * cells
            total = jnp.sum(total, axis=0, keepdims=True)
            energy[pl.ds(m, 1), :] = total[:, :128] + total[:, 128:]
            faces_of(lambda m, i: u[m, i, pl.ds(1, nx)], uface, m)
            return carry

        lax.fori_loop(g * GROUP, (g + 1) * GROUP, u_mode, 0)

    def e_copy(index, peer, dst):
        return pltpu.make_async_remote_copy(
            src_ref=energy.at[pl.ds(modes * (0 if index < nc - 1 else 1 if index < nc + zs - 2 else 2), modes)],
            dst_ref=dst, send_sem=es_sem.at[index], recv_sem=er_sem.at[index], device_id=peer, device_id_type=MESH)

    ones = [e_copy(k, first[k], round_one.at[k]) for k in range(nc - 1)]
    twos = [e_copy(nc - 1 + k, second[k], round_two.at[k]) for k in range(zs - 1)]
    threes = [e_copy(nc + zs - 2 + k, third[k], round_three.at[k]) for k in range(rest - 1)]

    def v_faces(g):
        v_load(g).wait()

        def v_mode(m, carry):
            faces_of(lambda m, i: v[m, i], vface, m)
            return carry

        lax.fori_loop(g * GROUP, (g + 1) * GROUP, v_mode, 0)

    def finish(copies, slots, src):
        total = energy[pl.ds(modes * src, modes), :]
        for k, copy in enumerate(copies):
            copy.wait_recv()
            total = total + slots[k]
        return total

    for copy in ones:
        copy.start()
    v_faces(0)
    energy[pl.ds(modes, modes), :] = finish(ones, round_one, 0)
    for copy in twos:
        copy.start()

    width = 3 * kv
    lane = iota((ny, width), 1)
    row = iota((ny, width), 0)
    lane_row = lax.rem(lane, ny)
    lane_var = lax.rem(lane, kv) // ny
    same = jnp.where(lane_row == row, 1.0, 0.0)
    nxt = jnp.where(lane_row == row + 1, 1.0, 0.0)
    prv = jnp.where(lane_row == row - 1, 1.0, 0.0)
    kinds = ((0, same), (1, nxt - same), (1, same - prv), (2, same), (1, same))
    for k, (d, stencil) in enumerate(kinds):
        for j in range(nv):
            coefs = jnp.zeros((ny, width), F32)
            for i in range(nv):
                coefs = jnp.where(lane_var == i, mix[d, i, j], coefs)
            mat0[pl.ds((k * nv + j) * ny, ny), :] = coefs * stencil
    high = mat0[...].astype(BF16)
    low = (mat0[...] - high.astype(F32)).astype(BF16)
    mat2[...] = jnp.where(iota(mat0.shape, 1) < 2 * kv, high.astype(F32), low.astype(F32)).astype(BF16)

    v_faces(1)
    energy[pl.ds(2 * modes, modes), :] = finish(twos, round_two, 1)
    for copy in threes:
        copy.start()
    v_faces(2)

    cell_load.wait()
    base_load.wait()
    kind_of = cell[...]
    weight[...] = jnp.where(kind_of == 0, 1.0, jnp.where(kind_of == 1, 0.5, 0.0)).astype(F32)
    for side in (0, 1):
        for x in range(nx):
            bface[side, :, pl.ds(x, 1), :] = base[:, 1 + x, pl.ds((ny - 1) * side, 1), :]

    def base_plane(x, carry):
        for j in range(nv):
            base_dz[j, x] = diff_lanes(base[j, 1 + x])
        return carry

    lax.fori_loop(0, nx, base_plane, 0)
    v_faces(3)

    cells_all = nc * nn * nv * nx * ny * nz
    total = jnp.sum(finish(threes, round_three, 2), axis=1, keepdims=True)
    send(x_links[0], has_x)
    send(y_links[4], has_y)
    send(x_links[1], has_x)
    send(y_links[0], has_y)
    amp[...] = jnp.broadcast_to(lax.rsqrt(total / cells_all + 1e-06) / modes, amp.shape)

    def mode_matrix(m, carry):
        scaled = mat0[:, pl.ds(0, 2 * kv)] * amp[pl.ds(m, 1), pl.ds(0, 2 * kv)]
        big = scaled.astype(BF16).astype(F32)
        mats[m] = jnp.where(iota(scaled.shape, 1) < kv, big, scaled - big).astype(BF16)
        return carry

    lax.fori_loop(0, modes, mode_matrix, 0)

    sface[...] = jnp.zeros(sface.shape, F32)
    sx[:, 1] = jnp.zeros((nv, ny, nz), F32)
    sx[:, 2] = jnp.zeros((nv, ny, nz), F32)

    def face_group(g, carry):
        m0 = g * GROUP
        for s in (0, 1):
            x = 1 + (nx - 1) * s
            for k in range(GROUP):
                rows = vface[s, pick[m0 + k]].reshape(kv, nz)
                wface[s, m0 + k] = dot(mats[m0 + k, pl.ds(4 * kv, kv), :], jnp.concatenate([rows, rows], axis=0))
                rows = v[pick[m0 + k], :, x - 1].reshape(kv, nz)
                w_scr[s, k, pl.ds(0, kv), :] = dot(mats[m0 + k, pl.ds(0, kv), :], jnp.concatenate([rows, rows], axis=0))
        for s in (0, 1):
            x = 1 + (nx - 1) * s
            for j in range(nv):
                r = pl.ds(j * ny, ny)
                at_face, at_end = sface[s, j], sx[j, 1 + s]
                for k in range(GROUP):
                    at_face = at_face + wface[s, m0 + k, pl.ds(j * nx, nx), :] * uface[s, m0 + k, j].astype(F32)
                    at_end = at_end + w_scr[s, k, r, :] * u[m0 + k, j, x].astype(F32)
                sface[s, j] = at_face
                sx[j, 1 + s] = at_end
        return carry

    lax.fori_loop(0, groups, face_group, 0)
    send(x_links[2], has_x)
    send(y_links[1], has_y)

    def mix_part(x, g, slot, k):
        m0 = g * GROUP
        if k == GROUP:
            du_scr[slot] = dot(u[pl.ds(m0, GROUP), :, x].reshape(GROUP * kv, nz), circ[...])
        elif k < GROUP:
            rows = v[pick[m0 + k], :, x - 1].reshape(kv, nz)
            w_scr[slot, k] = dot(mats[m0 + k, pl.ds(0, 4 * kv), :], jnp.concatenate([rows, rows], axis=0))

    def mix_group(x, g, slot):
        for k in range(GROUP + 1):
            mix_part(x, g, slot, k)

    def plane_of(t):
        return lax.rem(t + 1, nx) + 1

    def plane(t, carry):
        x = plane_of(t)
        for g in range(groups):
            slot = g % 2
            for j in range(nv):
                if g < groups - 1:
                    mix_part(x, g + 1, 1 - slot, j)
                else:
                    mix_part(plane_of(t + 1), 0, 1 - slot, j)
                if g == 0:
                    q = s_x = s_z = up = down = jnp.zeros((ny, nz), F32)
                else:
                    q, s_x, s_z, up, down = (acc[i, j] for i in range(5))
                for k in range(GROUP):
                    m = g * GROUP + k
                    here = u[m, j, x].astype(F32)
                    dx = u[m, j, x + 1].astype(F32) - u[m, j, x - 1].astype(F32)
                    dz = du_scr[slot, pl.ds(k * kv + j * ny, ny), :]
                    wx, wp, wm, wz = (w_scr[slot, k, pl.ds(i * kv + j * ny, ny), :] for i in range(4))
                    q = q + dx * wx + dz * wz
                    s_x = s_x + here * wx
                    s_z = s_z + here * wz
                    up = up + here * wm
                    down = down + here * wp
                if g < groups - 1:
                    for i, value in enumerate((q, s_x, s_z, up, down)):
                        acc[i, j] = value
                else:
                    grad[j, x - 1] = q - diff_lanes(s_z) - rows_up(up) - rows_down(down)
                    sx_all[j, x - 1] = s_x
        return carry

    mix_group(plane_of(0), 0, 0)
    lax.fori_loop(0, nx - 2, plane, 0)
    receive(x_links[0], has_x)
    lax.fori_loop(nx - 2, nx, plane, 0)

    receive(y_links[4], has_y)
    fterm[...] = jnp.zeros(fterm.shape, F32)

    def cross_mode(m, carry):
        for s in (0, 1):
            fterm[s] += wface[s, m].reshape(nv, nx, nz) * uhalo[s, m].astype(F32)
        return carry

    lax.fori_loop(0, modes, cross_mode, 0)
    receive(y_links[1], has_y)
    receive(x_links[2], has_x)
    fterm[0] = shalo[0] - fterm[0]
    fterm[1] = fterm[1] - shalo[1]

    def add_rows(target, x0):
        for side in (0, 1):
            for x in range(nx):
                end = pl.ds((ny - 1) * side, 1)
                target[:, x + x0, end, :] = target[:, x + x0, end, :] + fterm[side, :, pl.ds(x, 1), :]

    def grad_plane(x, carry):
        for j in range(nv):
            grad[j, x] = grad[j, x] - (sx_all[j, x + 1] - sx_all[j, x - 1])
        return carry

    for j in range(nv):
        grad[j, 0] = grad[j, 0] - (sx_all[j, 1] - sx[j, 0])
        grad[j, nx - 1] = grad[j, nx - 1] - (sx[j, 3] - sx_all[j, nx - 2])
    lax.fori_loop(1, nx - 1, grad_plane, 0, unroll=2)
    add_rows(grad, 0)

    def apply(slot, source, target):
        def weigh(x, carry):
            for j in range(nv):
                field[slot, j, x + 1] = weight[x] * source[j, x]
            return carry

        lax.fori_loop(0, nx, weigh, 0, unroll=2)
        for side in (0, 1):
            for x in range(nx):
                ysend[slot, side, :, pl.ds(x, 1), :] = field[slot, :, 1 + x, pl.ds((ny - 1) * side, 1), :]
        send(x_links[3 + slot], has_x)
        send(y_links[2 + slot], has_y)


        def mixed(x, carry):
            wall[x] = dot(mat2[pl.ds(0, 4 * kv), :], split3(field[slot, :, x].reshape(kv, nz)))
            return carry

        lax.fori_loop(1, nx + 1, mixed, 0, unroll=4)
        own = [dot(mat2[pl.ds(4 * kv, kv), :], split3(ysend[slot, s].reshape(kv, nz))) for s in (0, 1)]
        for s in (0, 1):
            wface[s, 0] = own[s]

        def result_plane(x, carry):
            for j in range(nv):
                r = pl.ds(j * ny, ny)
                wx = wall[x, r, :]
                wp, wm, wz = (wall[x, pl.ds(t * kv + j * ny, ny), :] for t in (1, 2, 3))
                here = base[j, x]
                value = base[j, x + 1] * (wx - wall[x + 1, r, :]) - base[j, x - 1] * (wx - wall[x - 1, r, :])
                value = value + base_dz[j, x - 1] * wz - diff_lanes(here * wz)
                target[j, x - 1] = value - rows_up(here * wm) - rows_down(here * wp)
            return carry

        lax.fori_loop(2, nx, result_plane, 0, unroll=2)
        if slot == 0:
            receive(x_links[1], has_x)
            receive(y_links[0], has_y)
        receive(x_links[3 + slot], has_x)
        receive(y_links[2 + slot], has_y)
        for x in (0, nx + 1):
            wall[x, pl.ds(0, kv), :] = dot(mat2[pl.ds(0, kv), :], split3(field[slot, :, x].reshape(kv, nz)))
        lax.fori_loop(0, 2, lambda s, carry: result_plane(1 + (nx - 1) * s, carry), 0, unroll=2)
        for s in (0, 1):
            far = dot(mat2[pl.ds(4 * kv, kv), :], split3(yhalo[slot, s].reshape(kv, nz)))
            change = (far - wface[s, 0]).reshape(nv, nx, nz) * bhalo[s]
            fterm[s] = change if s == 0 else -change
        add_rows(target, 0)

    apply(0, grad, result)
    apply(1, result, grad)
    store = pltpu.make_async_copy(grad, out_hbm, out_sem)
    store.start()
    for link in x_links:
        drain(link, has_x)
    for link in y_links:
        drain(link, has_y)
    for copy in ones + twos + threes:
        copy.wait_send()
    store.wait()


def per_device(u, v, base, cell, pick, mix, *, interpret=False):
    modes, nv, nx, ny, nz = u.shape
    nc, nn = lax.axis_size("chord"), lax.axis_size("normal")
    kv = nv * ny
    groups = modes // GROUP
    vm = pltpu.VMEM
    any_space = pl.BlockSpec(memory_space=pl.ANY)
    smem = pl.BlockSpec(memory_space=pltpu.SMEM)
    return pl.pallas_call(
        functools.partial(kernel, (nc, nn, modes, nv, nx, ny, nz)),
        out_shape=jax.ShapeDtypeStruct(base.shape, F32),
        in_specs=[any_space] * 4 + [smem] * 2,
        out_specs=any_space,
        scratch_shapes=[
            vm((modes, nv, nx + 2, ny, nz), BF16),
            vm((modes, nv, nx, ny, nz), BF16),
            vm((nv, nx + 2, ny, nz), F32),
            vm((nx, ny, nz), jnp.int32),
            vm((2, modes, nv, nx, nz), BF16),
            vm((2, modes, nv, nx, nz), BF16),
            vm((2, modes, nv, nx, nz), BF16),
            vm((2, modes, kv, nz), F32),
            vm((modes, 5 * kv, 2 * kv), BF16),
            vm((5 * kv, 3 * kv), BF16),
            vm((5 * kv, 3 * kv), F32),
            vm((2 * nx, nx * ny), BF16),
            vm((nz, nz), BF16),
            vm((2, GROUP, 4 * kv, nz), F32),
            vm((2, GROUP * kv, nz), F32),
            vm((5, nv, ny, nz), F32),
            vm((nv, nx, ny, nz), F32),
            vm((nv, 4, ny, nz), F32),
            vm((nv, nx, ny, nz), F32),
            vm((2, nv, nx, nz), F32),
            vm((2, nv, nx, nz), F32),
            vm((2, 2, nv, nx, nz), F32),
            vm((2, 2, nv, nx, nz), F32),
            vm((2, nv, nx + 2, ny, nz), F32),
            vm((nx + 2, 4 * kv, nz), F32),
            vm((nv, nx, ny, nz), F32),
            vm((2, nv, nx, nz), F32),
            vm((2, nv, nx, nz), F32),
            vm((2, nv, nx, nz), F32),
            vm((3 * modes, 128), F32),
            vm((nc - 1, modes, 128), F32),
            vm((3, modes, 128), F32),
            vm((max(nn // 4 - 1, 1), modes, 128), F32),
            vm((modes, 256), F32),
            vm((nx, ny, nz), F32),
            vm((nv, nx, ny, nz), F32),
            pltpu.SemaphoreType.DMA((2 * groups + 2,)),
            pltpu.SemaphoreType.DMA((5, 2)),
            pltpu.SemaphoreType.DMA((5, 2)),
            pltpu.SemaphoreType.DMA((5, 2)),
            pltpu.SemaphoreType.DMA((5, 2)),
            pltpu.SemaphoreType.DMA((nc + nn // 4 + 1,)),
            pltpu.SemaphoreType.DMA((nc + nn // 4 + 1,)),
            pltpu.SemaphoreType.DMA,
        ],
        compiler_params=pltpu.CompilerParams(
            collective_id=0, has_side_effects=True, vmem_limit_bytes=60 * 2**20),
    )(u, v, base, cell, pick, mix)


def solution(mesh):
    return jax.shard_map(
        per_device,
        mesh=mesh,
        in_specs=(
            P(None, None, "chord", "normal", None),
            P(None, None, "chord", "normal", None),
            P(None, "chord", "normal", None),
            P("chord", "normal", None),
            P(),
            P(),
        ),
        out_specs=P(None, "chord", "normal", None),
        check_vma=False,
    )
```

```python
import functools

import jax
import jax.numpy as jnp
from jax import lax
from jax.experimental import pallas as pl
from jax.experimental.pallas import tpu as pltpu
from jax.sharding import PartitionSpec as P

MESH = pl.DeviceIdType.MESH
F32 = jnp.float32
BF16 = jnp.bfloat16
GROUP = 4
MG = 2


def iota(shape, dim):
    return lax.broadcasted_iota(jnp.int32, shape, dim)


def diff_lanes(x):
    lanes = x.shape[-1]
    return pltpu.roll(x, lanes - 1, 1) - pltpu.roll(x, 1, 1)


def rows_up(x):
    rows = x.shape[0]
    return jnp.where(iota(x.shape, 0) == rows - 1, 0.0, pltpu.roll(x, rows - 1, 0))


def rows_down(x):
    return jnp.where(iota(x.shape, 0) == 0, 0.0, pltpu.roll(x, 1, 0))


def split3(x):
    high = x.astype(BF16)
    low = (x - high.astype(F32)).astype(BF16)
    return jnp.concatenate([high, low, high], axis=0)


def dot(a, b):
    return jnp.dot(a, b, preferred_element_type=F32)


def kernel(
    sizes,
    u_hbm, v_hbm, base_hbm, cell_hbm, mix_hbm, pick,
    out_hbm,
    u, v, base, cell, mix, uface, vface, uhalo, wface, mats, mat2, mat0, select, circ,
    w_scr, du_scr, acc, grad, sx, sx_all, sface, shalo, ysend, yhalo, field, wall, base_dz, bface, bhalo,
    fterm, energy, round_one, round_two, round_three, amp, weight, result,
    load_sem, xs_sem, xr_sem, ys_sem, yr_sem, es_sem, er_sem, out_sem,
):
    nc, nn, modes, nv, nx, ny, nz = sizes
    kv = nv * ny
    c, n = lax.axis_index("chord"), lax.axis_index("normal")
    has_x = (c > 0, c < nc - 1)
    has_y = (n > 0, n < nn - 1)
    half = nn // 2
    far_y = (n == half, n == half - 1)
    near_y = tuple(jnp.logical_and(a, jnp.logical_not(b)) for a, b in zip(has_y, far_y))
    step = (-1, 1)
    zs, rest = 4, nn // 4
    groups = modes // GROUP

    def u_load(g):
        s = pl.ds(g * GROUP, GROUP)
        return pltpu.make_async_copy(u_hbm.at[s], u.at[s, :, pl.ds(1, nx)], load_sem.at[g])

    def v_load(g):
        s = pl.ds(g * GROUP, GROUP)
        return pltpu.make_async_copy(v_hbm.at[s], v.at[s], load_sem.at[groups + g])

    base_load = pltpu.make_async_copy(base_hbm, base.at[:, pl.ds(1, nx)], load_sem.at[2 * groups])
    cell_load = pltpu.make_async_copy(cell_hbm, cell, load_sem.at[2 * groups + 1])
    mix_load = pltpu.make_async_copy(mix_hbm, mix, load_sem.at[2 * groups + 2])
    mix_load.start()
    for g in range(groups):
        u_load(g).start()
    base_load.start()
    cell_load.start()
    for g in range(groups):
        v_load(g).start()

    first = [(lax.rem(c + k, nc), n) for k in range(1, nc)]
    second = [(c, n // zs * zs + lax.rem(lax.rem(n, zs) + k, zs)) for k in range(1, zs)]
    third = [(c, lax.rem(n // zs + k, rest) * zs + lax.rem(n, zs)) for k in range(1, rest)]
    around = [(c, lax.rem(n + 1, nn)), (c, lax.rem(n + nn - 1, nn))]
    barrier = pltpu.get_barrier_semaphore()
    peers = first + second + third + around
    for peer in peers:
        pl.semaphore_signal(barrier, inc=1, device_id=peer, device_id_type=MESH)

    @pl.when(c == 0)
    def _():
        u[:, :, 0] = jnp.zeros((modes, nv, ny, nz), BF16)
        base[:, 0] = jnp.zeros((nv, ny, nz), F32)
        sx[:, 0] = jnp.zeros((nv, ny, nz), F32)
        field[0, :, 0] = jnp.zeros((nv, ny, nz), F32)
        field[1, :, 0] = jnp.zeros((nv, ny, nz), F32)

    @pl.when(c == nc - 1)
    def _():
        u[:, :, nx + 1] = jnp.zeros((modes, nv, ny, nz), BF16)
        base[:, nx + 1] = jnp.zeros((nv, ny, nz), F32)
        sx[:, 3] = jnp.zeros((nv, ny, nz), F32)
        field[0, :, nx + 1] = jnp.zeros((nv, ny, nz), F32)
        field[1, :, nx + 1] = jnp.zeros((nv, ny, nz), F32)

    for side, at_edge in ((0, n == 0), (1, n == nn - 1)):
        @pl.when(at_edge)
        def _():
            uhalo[side] = jnp.zeros((modes, nv, nx, nz), BF16)
            bhalo[side] = jnp.zeros((nv, nx, nz), F32)
            shalo[side] = jnp.zeros((nv, nx, nz), F32)
            yhalo[0, side] = jnp.zeros((nv, nx, nz), F32)
            yhalo[1, side] = jnp.zeros((nv, nx, nz), F32)

    pl.semaphore_wait(barrier, len(peers))

    def x_copy(kind, way, src, dst):
        return pltpu.make_async_remote_copy(
            src_ref=src, dst_ref=dst, send_sem=xs_sem.at[kind, way], recv_sem=xr_sem.at[kind, 1 - way],
            device_id=(lax.rem(c + step[way] + nc, nc), n), device_id_type=MESH)

    def y_copy(kind, way, src, dst):
        return pltpu.make_async_remote_copy(
            src_ref=src, dst_ref=dst, send_sem=ys_sem.at[kind, way], recv_sem=yr_sem.at[kind, 1 - way],
            device_id=(c, lax.rem(n + step[way] + nn, nn)), device_id_type=MESH)

    x_links = [
        lambda w: x_copy(0, w, u_hbm.at[:, :, (nx - 1) * w], u.at[:, :, (nx + 1) * (1 - w)]),
        lambda w: x_copy(1, w, base_hbm.at[:, (nx - 1) * w], base.at[:, (nx + 1) * (1 - w)]),
        lambda w: x_copy(2, w, sx.at[:, 1 + w], sx.at[:, 3 * (1 - w)]),
        lambda w: x_copy(3, w, field.at[0, :, 1 + (nx - 1) * w], field.at[0, :, (nx + 1) * (1 - w)]),
        lambda w: x_copy(4, w, field.at[1, :, 1 + (nx - 1) * w], field.at[1, :, (nx + 1) * (1 - w)]),
    ]
    y_links = [
        lambda w: y_copy(0, w, bface.at[w], bhalo.at[1 - w]),
        lambda w: y_copy(1, w, sface.at[w], shalo.at[1 - w]),
        lambda w: y_copy(2, w, ysend.at[0, w], yhalo.at[0, 1 - w]),
        lambda w: y_copy(3, w, ysend.at[1, w], yhalo.at[1, 1 - w]),
        lambda w: y_copy(4, w, uface.at[w, pl.ds(0, GROUP)], uhalo.at[1 - w, pl.ds(0, GROUP)]),
        lambda w: y_copy(5, w, uface.at[w, pl.ds(GROUP, modes - GROUP)], uhalo.at[1 - w, pl.ds(GROUP, modes - GROUP)]),
    ]

    def send(link, has):
        for w in (0, 1):
            @pl.when(has[w])
            def _():
                link(w).start()

    def receive(link, has):
        for side in (0, 1):
            @pl.when(has[side])
            def _():
                link(1 - side).wait_recv()

    def drain(link, has):
        for w in (0, 1):
            @pl.when(has[w])
            def _():
                link(w).wait_send()

    pick_row = iota((2 * nx, nx * ny), 0)
    from_row = iota((2 * nx, nx * ny), 1)
    wanted = jnp.where(pick_row < nx, pick_row * ny, (pick_row - nx) * ny + ny - 1)
    select[...] = jnp.where(from_row == wanted, 1.0, 0.0).astype(BF16)
    lane_in, lane_out = iota((nz, nz), 0), iota((nz, nz), 1)
    ahead = jnp.where(lane_out == nz - 1, 0, lane_out + 1)
    behind = jnp.where(lane_out == 0, nz - 1, lane_out - 1)
    circ[...] = (jnp.where(lane_in == ahead, 1.0, 0.0) - jnp.where(lane_in == behind, 1.0, 0.0)).astype(BF16)

    def faces_of(block, faces, m):
        for i in range(nv):
            both = dot(select[...], block(m, i).reshape(nx * ny, nz))
            faces[0, m, i] = both[:nx].astype(BF16)
            faces[1, m, i] = both[nx:].astype(BF16)

    for g in range(groups):
        u_load(g).wait()

        def u_mode(m, carry):
            total = jnp.zeros((ny, nz), F32)
            for i in range(nv):
                for x in range(nx):
                    cells = u[m, i, 1 + x].astype(F32)
                    total = total + cells * cells
            total = jnp.sum(total, axis=0, keepdims=True)
            energy[pl.ds(m, 1), :] = total[:, :128] + total[:, 128:]
            faces_of(lambda m, i: u[m, i, pl.ds(1, nx)], uface, m)
            return carry

        lax.fori_loop(g * GROUP, (g + 1) * GROUP, u_mode, 0)
        if g == 0:
            send(y_links[4], far_y)

    def e_copy(index, peer, dst):
        return pltpu.make_async_remote_copy(
            src_ref=energy.at[pl.ds(modes * (0 if index < nc - 1 else 1 if index < nc + zs - 2 else 2), modes)],
            dst_ref=dst, send_sem=es_sem.at[index], recv_sem=er_sem.at[index], device_id=peer, device_id_type=MESH)

    ones = [e_copy(k, first[k], round_one.at[k]) for k in range(nc - 1)]
    twos = [e_copy(nc - 1 + k, second[k], round_two.at[k]) for k in range(zs - 1)]
    threes = [e_copy(nc + zs - 2 + k, third[k], round_three.at[k]) for k in range(rest - 1)]

    def v_faces(g):
        v_load(g).wait()

        def v_mode(m, carry):
            faces_of(lambda m, i: v[m, i], vface, m)
            return carry

        lax.fori_loop(g * GROUP, (g + 1) * GROUP, v_mode, 0, unroll=2)

    def finish(copies, slots, src):
        total = energy[pl.ds(modes * src, modes), :]
        for k, copy in enumerate(copies):
            copy.wait_recv()
            total = total + slots[k]
        return total

    for copy in ones:
        copy.start()
    v_faces(0)
    energy[pl.ds(modes, modes), :] = finish(ones, round_one, 0)
    for copy in twos:
        copy.start()

    mix_load.wait()
    width = 3 * kv
    lane = iota((ny, width), 1)
    row = iota((ny, width), 0)
    lane_row = lax.rem(lane, ny)
    lane_var = lax.rem(lane, kv) // ny
    same = jnp.where(lane_row == row, 1.0, 0.0)
    nxt = jnp.where(lane_row == row + 1, 1.0, 0.0)
    prv = jnp.where(lane_row == row - 1, 1.0, 0.0)
    kinds = ((0, same), (1, nxt - same), (1, same - prv), (2, same), (1, same))
    table = [mix[i] for i in range(nv)]
    for k, (d, stencil) in enumerate(kinds):
        for j in range(nv):
            coefs = jnp.zeros((ny, width), F32)
            for i in range(nv):
                coefs = jnp.where(lane_var == i, table[i][d : d + 1, j : j + 1], coefs)
            mat0[pl.ds((k * nv + j) * ny, ny), :] = coefs * stencil
    high = mat0[...].astype(BF16)
    low = (mat0[...] - high.astype(F32)).astype(BF16)
    mat2[...] = jnp.where(iota(mat0.shape, 1) < 2 * kv, high.astype(F32), low.astype(F32)).astype(BF16)

    v_faces(1)
    energy[pl.ds(2 * modes, modes), :] = finish(twos, round_two, 1)
    for copy in threes:
        copy.start()
    v_faces(2)

    cell_load.wait()
    base_load.wait()
    kind_of = cell[...]
    weight[...] = jnp.where(kind_of == 0, 1.0, jnp.where(kind_of == 1, 0.5, 0.0)).astype(F32)
    for side in (0, 1):
        for x in range(nx):
            bface[side, :, pl.ds(x, 1), :] = base[:, 1 + x, pl.ds((ny - 1) * side, 1), :]

    def base_plane(x, carry):
        for j in range(nv):
            base_dz[j, x] = diff_lanes(base[j, 1 + x])
        return carry

    lax.fori_loop(0, nx, base_plane, 0)
    v_faces(3)

    cells_all = nc * nn * nv * nx * ny * nz
    total = jnp.sum(finish(threes, round_three, 2), axis=1, keepdims=True)
    send(y_links[5], far_y)
    send(x_links[0], has_x)
    send(y_links[4], near_y)
    send(y_links[5], near_y)
    send(x_links[1], has_x)
    send(y_links[0], has_y)
    amp[...] = jnp.broadcast_to(lax.rsqrt(total / cells_all + 1e-06) / modes, amp.shape)

    def mode_matrix(m, carry):
        scaled = mat0[:, pl.ds(0, 2 * kv)] * amp[pl.ds(m, 1), pl.ds(0, 2 * kv)]
        big = scaled.astype(BF16).astype(F32)
        mats[m] = jnp.where(iota(scaled.shape, 1) < kv, big, scaled - big).astype(BF16)
        return carry

    lax.fori_loop(0, modes, mode_matrix, 0)

    sface[...] = jnp.zeros(sface.shape, F32)
    sx[:, 1] = jnp.zeros((nv, ny, nz), F32)
    sx[:, 2] = jnp.zeros((nv, ny, nz), F32)

    def face_group(g, carry):
        m0 = g * GROUP
        for s in (0, 1):
            x = 1 + (nx - 1) * s
            for k in range(GROUP):
                rows = vface[s, pick[m0 + k]].reshape(kv, nz)
                wface[s, m0 + k] = dot(mats[m0 + k, pl.ds(4 * kv, kv), :], jnp.concatenate([rows, rows], axis=0))
                rows = v[pick[m0 + k], :, x - 1].reshape(kv, nz)
                w_scr[s, k, pl.ds(0, kv), :] = dot(mats[m0 + k, pl.ds(0, kv), :], jnp.concatenate([rows, rows], axis=0))
        for s in (0, 1):
            x = 1 + (nx - 1) * s
            for j in range(nv):
                r = pl.ds(j * ny, ny)
                at_face, at_end = sface[s, j], sx[j, 1 + s]
                for k in range(GROUP):
                    at_face = at_face + wface[s, m0 + k, pl.ds(j * nx, nx), :] * uface[s, m0 + k, j].astype(F32)
                    at_end = at_end + w_scr[s, k, r, :] * u[m0 + k, j, x].astype(F32)
                sface[s, j] = at_face
                sx[j, 1 + s] = at_end
        return carry

    lax.fori_loop(0, groups, face_group, 0)
    send(x_links[2], has_x)
    send(y_links[1], has_y)

    def mix_part(x, g, slot, k):
        m0 = g * MG
        if k == MG:
            du_scr[slot] = dot(u[pl.ds(m0, MG), :, x].reshape(MG * kv, nz), circ[...])
        elif k < MG:
            rows = v[pick[m0 + k], :, x - 1].reshape(kv, nz)
            w_scr[slot, k] = dot(mats[m0 + k, pl.ds(0, 4 * kv), :], jnp.concatenate([rows, rows], axis=0))

    def mix_group(x, g, slot):
        for k in range(MG + 1):
            mix_part(x, g, slot, k)

    def plane_of(t):
        return lax.rem(t + 1, nx) + 1

    def plane(t, carry):
        x = plane_of(t)
        for g in range((modes // MG)):
            slot = g % 2
            for j in range(nv):
                for part in range(j, MG + 1, nv):
                    if g < (modes // MG) - 1:
                        mix_part(x, g + 1, 1 - slot, part)
                    else:
                        mix_part(plane_of(t + 1), 0, 1 - slot, part)
                for h in (0, 1):
                    z = pl.ds(128 * h, 128)
                    if g == 0:
                        q = s_x = s_z = up = down = jnp.zeros((ny, 128), F32)
                    else:
                        q, s_x, s_z, up, down = (acc[i, j, :, z] for i in range(5))
                    for k in range(MG):
                        m = g * MG + k
                        here = u[m, j, x, :, z].astype(F32)
                        dx = u[m, j, x + 1, :, z].astype(F32) - u[m, j, x - 1, :, z].astype(F32)
                        dz = du_scr[slot, pl.ds(k * kv + j * ny, ny), z]
                        wx, wp, wm, wz = (w_scr[slot, k, pl.ds(i * kv + j * ny, ny), z] for i in range(4))
                        q = q + dx * wx + dz * wz
                        s_x = s_x + here * wx
                        s_z = s_z + here * wz
                        up = up + here * wm
                        down = down + here * wp
                    for i, value in enumerate((q, s_x, s_z, up, down)):
                        acc[i, j, :, z] = value
                if g == (modes // MG) - 1:
                    grad[j, x - 1] = acc[0, j] - diff_lanes(acc[2, j]) - rows_up(acc[3, j]) - rows_down(acc[4, j])
                    sx_all[j, x - 1] = acc[1, j]
        return carry

    mix_group(plane_of(0), 0, 0)
    lax.fori_loop(0, nx - 2, plane, 0)
    receive(x_links[0], has_x)
    lax.fori_loop(nx - 2, nx, plane, 0)

    receive(y_links[4], has_y)
    receive(y_links[5], has_y)
    fterm[...] = jnp.zeros(fterm.shape, F32)

    def cross_mode(m, carry):
        for s in (0, 1):
            fterm[s] += wface[s, m].reshape(nv, nx, nz) * uhalo[s, m].astype(F32)
        return carry

    lax.fori_loop(0, modes, cross_mode, 0)
    receive(y_links[1], has_y)
    receive(x_links[2], has_x)
    fterm[0] = shalo[0] - fterm[0]
    fterm[1] = fterm[1] - shalo[1]

    def add_rows(target, x0):
        for side in (0, 1):
            for x in range(nx):
                end = pl.ds((ny - 1) * side, 1)
                target[:, x + x0, end, :] = target[:, x + x0, end, :] + fterm[side, :, pl.ds(x, 1), :]

    def grad_plane(x, carry):
        for j in range(nv):
            grad[j, x] = grad[j, x] - (sx_all[j, x + 1] - sx_all[j, x - 1])
        return carry

    for j in range(nv):
        grad[j, 0] = grad[j, 0] - (sx_all[j, 1] - sx[j, 0])
        grad[j, nx - 1] = grad[j, nx - 1] - (sx[j, 3] - sx_all[j, nx - 2])
    lax.fori_loop(1, nx - 1, grad_plane, 0, unroll=2)
    add_rows(grad, 0)

    def apply(slot, source, target):
        def weigh(x, carry):
            for j in range(nv):
                field[slot, j, x + 1] = weight[x] * source[j, x]
            return carry

        lax.fori_loop(0, nx, weigh, 0, unroll=2)
        for side in (0, 1):
            for x in range(nx):
                ysend[slot, side, :, pl.ds(x, 1), :] = field[slot, :, 1 + x, pl.ds((ny - 1) * side, 1), :]
        send(x_links[3 + slot], has_x)
        send(y_links[2 + slot], has_y)


        def mixed(x, carry):
            wall[x] = dot(mat2[pl.ds(0, 4 * kv), :], split3(field[slot, :, x].reshape(kv, nz)))
            return carry

        lax.fori_loop(1, nx + 1, mixed, 0, unroll=4)
        own = [dot(mat2[pl.ds(4 * kv, kv), :], split3(ysend[slot, s].reshape(kv, nz))) for s in (0, 1)]
        for s in (0, 1):
            wface[s, 0] = own[s]

        def result_plane(x, carry):
            for j in range(nv):
                r = pl.ds(j * ny, ny)
                wx = wall[x, r, :]
                wp, wm, wz = (wall[x, pl.ds(t * kv + j * ny, ny), :] for t in (1, 2, 3))
                here = base[j, x]
                value = base[j, x + 1] * (wx - wall[x + 1, r, :]) - base[j, x - 1] * (wx - wall[x - 1, r, :])
                value = value + base_dz[j, x - 1] * wz - diff_lanes(here * wz)
                target[j, x - 1] = value - rows_up(here * wm) - rows_down(here * wp)
            return carry

        lax.fori_loop(2, nx, result_plane, 0, unroll=2)
        if slot == 0:
            receive(x_links[1], has_x)
            receive(y_links[0], has_y)
        receive(x_links[3 + slot], has_x)
        receive(y_links[2 + slot], has_y)
        for x in (0, nx + 1):
            wall[x, pl.ds(0, kv), :] = dot(mat2[pl.ds(0, kv), :], split3(field[slot, :, x].reshape(kv, nz)))
        lax.fori_loop(0, 2, lambda s, carry: result_plane(1 + (nx - 1) * s, carry), 0, unroll=2)
        for s in (0, 1):
            far = dot(mat2[pl.ds(4 * kv, kv), :], split3(yhalo[slot, s].reshape(kv, nz)))
            change = (far - wface[s, 0]).reshape(nv, nx, nz) * bhalo[s]
            fterm[s] = change if s == 0 else -change
        add_rows(target, 0)

    apply(0, grad, result)
    apply(1, result, grad)
    store = pltpu.make_async_copy(grad, out_hbm, out_sem)
    store.start()
    for link in x_links:
        drain(link, has_x)
    for link in y_links:
        drain(link, has_y)
    for copy in ones + twos + threes:
        copy.wait_send()
    store.wait()


def per_device(u, v, base, cell, pick, mix, *, interpret=False):
    modes, nv, nx, ny, nz = u.shape
    nc, nn = lax.axis_size("chord"), lax.axis_size("normal")
    kv = nv * ny
    groups = modes // GROUP
    vm = pltpu.VMEM
    any_space = pl.BlockSpec(memory_space=pl.ANY)
    smem = pl.BlockSpec(memory_space=pltpu.SMEM)
    return pl.pallas_call(
        functools.partial(kernel, (nc, nn, modes, nv, nx, ny, nz)),
        out_shape=jax.ShapeDtypeStruct(base.shape, F32),
        in_specs=[any_space] * 5 + [smem],
        out_specs=any_space,
        scratch_shapes=[
            vm((modes, nv, nx + 2, ny, nz), BF16),
            vm((modes, nv, nx, ny, nz), BF16),
            vm((nv, nx + 2, ny, nz), F32),
            vm((nx, ny, nz), jnp.int32),
            vm((nv, 3, nv), F32),
            vm((2, modes, nv, nx, nz), BF16),
            vm((2, modes, nv, nx, nz), BF16),
            vm((2, modes, nv, nx, nz), BF16),
            vm((2, modes, kv, nz), F32),
            vm((modes, 5 * kv, 2 * kv), BF16),
            vm((5 * kv, 3 * kv), BF16),
            vm((5 * kv, 3 * kv), F32),
            vm((2 * nx, nx * ny), BF16),
            vm((nz, nz), BF16),
            vm((2, max(GROUP, MG), 4 * kv, nz), F32),
            vm((2, MG * kv, nz), F32),
            vm((5, nv, ny, nz), F32),
            vm((nv, nx, ny, nz), F32),
            vm((nv, 4, ny, nz), F32),
            vm((nv, nx, ny, nz), F32),
            vm((2, nv, nx, nz), F32),
            vm((2, nv, nx, nz), F32),
            vm((2, 2, nv, nx, nz), F32),
            vm((2, 2, nv, nx, nz), F32),
            vm((2, nv, nx + 2, ny, nz), F32),
            vm((nx + 2, 4 * kv, nz), F32),
            vm((nv, nx, ny, nz), F32),
            vm((2, nv, nx, nz), F32),
            vm((2, nv, nx, nz), F32),
            vm((2, nv, nx, nz), F32),
            vm((3 * modes, 128), F32),
            vm((nc - 1, modes, 128), F32),
            vm((3, modes, 128), F32),
            vm((max(nn // 4 - 1, 1), modes, 128), F32),
            vm((modes, 256), F32),
            vm((nx, ny, nz), F32),
            vm((nv, nx, ny, nz), F32),
            pltpu.SemaphoreType.DMA((2 * groups + 3,)),
            pltpu.SemaphoreType.DMA((5, 2)),
            pltpu.SemaphoreType.DMA((5, 2)),
            pltpu.SemaphoreType.DMA((6, 2)),
            pltpu.SemaphoreType.DMA((6, 2)),
            pltpu.SemaphoreType.DMA((nc + nn // 4 + 1,)),
            pltpu.SemaphoreType.DMA((nc + nn // 4 + 1,)),
            pltpu.SemaphoreType.DMA,
        ],
        compiler_params=pltpu.CompilerParams(
            collective_id=0, has_side_effects=True, vmem_limit_bytes=60 * 2**20),
    )(u, v, base, cell, mix.transpose(1, 0, 2), pick)


def solution(mesh):
    return jax.shard_map(
        per_device,
        mesh=mesh,
        in_specs=(
            P(None, None, "chord", "normal", None),
            P(None, None, "chord", "normal", None),
            P(None, "chord", "normal", None),
            P("chord", "normal", None),
            P(),
            P(),
        ),
        out_specs=P(None, "chord", "normal", None),
        check_vma=False,
    )
```

```python
import functools

import jax
import jax.numpy as jnp
from jax import lax
from jax.experimental import pallas as pl
from jax.experimental.pallas import tpu as pltpu
from jax.sharding import PartitionSpec as P

MESH = pl.DeviceIdType.MESH
F32 = jnp.float32
BF16 = jnp.bfloat16
GROUP = 4
MG = 2


def iota(shape, dim):
    return lax.broadcasted_iota(jnp.int32, shape, dim)


def diff_lanes(x):
    lanes = x.shape[-1]
    return pltpu.roll(x, lanes - 1, 1) - pltpu.roll(x, 1, 1)


def rows_up(x):
    rows = x.shape[0]
    return jnp.where(iota(x.shape, 0) == rows - 1, 0.0, pltpu.roll(x, rows - 1, 0))


def rows_down(x):
    return jnp.where(iota(x.shape, 0) == 0, 0.0, pltpu.roll(x, 1, 0))


def split3(x):
    high = x.astype(BF16)
    low = (x - high.astype(F32)).astype(BF16)
    return jnp.concatenate([high, low, high], axis=0)


def dot(a, b):
    return jnp.dot(a, b, preferred_element_type=F32)


def kernel(
    sizes,
    u_hbm, v_hbm, base_hbm, cell_hbm, mix_hbm, pick,
    out_hbm,
    u, v, base, cell, mix, uface, vface, uhalo, wface, mats, mat2, mat0, select, circ,
    w_scr, du_scr, acc, grad, sx, sx_all, sface, shalo, ysend, yhalo, field, wall, base_dz, bface, bhalo,
    fterm, relay, energy, round_one, round_two, round_three, amp, weight, result,
    load_sem, xs_sem, xr_sem, ys_sem, yr_sem, relay_send, relay_recv, es_sem, er_sem, out_sem,
):
    nc, nn, modes, nv, nx, ny, nz = sizes
    kv = nv * ny
    c, n = lax.axis_index("chord"), lax.axis_index("normal")
    has_x = (c > 0, c < nc - 1)
    has_y = (n > 0, n < nn - 1)
    half = nn // 2
    far_y = (n == half, n == half - 1)
    near_y = tuple(jnp.logical_and(a, jnp.logical_not(b)) for a, b in zip(has_y, far_y))
    step = (-1, 1)
    zs, rest = 4, nn // 4
    groups = modes // GROUP

    def u_load(g):
        s = pl.ds(g * GROUP, GROUP)
        return pltpu.make_async_copy(u_hbm.at[s], u.at[s, :, pl.ds(1, nx)], load_sem.at[g])

    def v_load(g):
        s = pl.ds(g * GROUP, GROUP)
        return pltpu.make_async_copy(v_hbm.at[s], v.at[s], load_sem.at[groups + g])

    base_load = pltpu.make_async_copy(base_hbm, base.at[:, pl.ds(1, nx)], load_sem.at[2 * groups])
    cell_load = pltpu.make_async_copy(cell_hbm, cell, load_sem.at[2 * groups + 1])
    mix_load = pltpu.make_async_copy(mix_hbm, mix, load_sem.at[2 * groups + 2])
    mix_load.start()
    for g in range(groups):
        u_load(g).start()
    base_load.start()
    cell_load.start()
    for g in range(groups):
        v_load(g).start()

    first = [(lax.rem(c + k, nc), n) for k in range(1, nc)]
    second = [(c, n // zs * zs + lax.rem(lax.rem(n, zs) + k, zs)) for k in range(1, zs)]
    third = [(c, lax.rem(n // zs + k, rest) * zs + lax.rem(n, zs)) for k in range(1, rest)]
    around = [(k, lax.rem(n + nn + d, nn)) for k in (c, lax.rem(c + nc // 2, nc)) for d in (1, -1)]
    barrier = pltpu.get_barrier_semaphore()
    peers = first + second + third + around
    for peer in peers:
        pl.semaphore_signal(barrier, inc=1, device_id=peer, device_id_type=MESH)

    @pl.when(c == 0)
    def _():
        u[:, :, 0] = jnp.zeros((modes, nv, ny, nz), BF16)
        base[:, 0] = jnp.zeros((nv, ny, nz), F32)
        sx[:, 0] = jnp.zeros((nv, ny, nz), F32)
        field[0, :, 0] = jnp.zeros((nv, ny, nz), F32)
        field[1, :, 0] = jnp.zeros((nv, ny, nz), F32)

    @pl.when(c == nc - 1)
    def _():
        u[:, :, nx + 1] = jnp.zeros((modes, nv, ny, nz), BF16)
        base[:, nx + 1] = jnp.zeros((nv, ny, nz), F32)
        sx[:, 3] = jnp.zeros((nv, ny, nz), F32)
        field[0, :, nx + 1] = jnp.zeros((nv, ny, nz), F32)
        field[1, :, nx + 1] = jnp.zeros((nv, ny, nz), F32)

    for side, at_edge in ((0, n == 0), (1, n == nn - 1)):
        @pl.when(at_edge)
        def _():
            uhalo[side] = jnp.zeros((modes, nv, nx, nz), BF16)
            bhalo[side] = jnp.zeros((nv, nx, nz), F32)
            shalo[side] = jnp.zeros((nv, nx, nz), F32)
            yhalo[0, side] = jnp.zeros((nv, nx, nz), F32)
            yhalo[1, side] = jnp.zeros((nv, nx, nz), F32)

    pl.semaphore_wait(barrier, len(peers))

    def x_copy(kind, way, src, dst):
        return pltpu.make_async_remote_copy(
            src_ref=src, dst_ref=dst, send_sem=xs_sem.at[kind, way], recv_sem=xr_sem.at[kind, 1 - way],
            device_id=(lax.rem(c + step[way] + nc, nc), n), device_id_type=MESH)

    def y_copy(kind, way, src, dst):
        return pltpu.make_async_remote_copy(
            src_ref=src, dst_ref=dst, send_sem=ys_sem.at[kind, way], recv_sem=yr_sem.at[kind, 1 - way],
            device_id=(c, lax.rem(n + step[way] + nn, nn)), device_id_type=MESH)

    late = pl.ds(2 * GROUP, modes - 2 * GROUP)

    x_links = [
        lambda w: x_copy(0, w, u_hbm.at[:, :, (nx - 1) * w], u.at[:, :, (nx + 1) * (1 - w)]),
        lambda w: x_copy(1, w, base_hbm.at[:, (nx - 1) * w], base.at[:, (nx + 1) * (1 - w)]),
        lambda w: x_copy(2, w, sx.at[:, 1 + w], sx.at[:, 3 * (1 - w)]),
        lambda w: x_copy(3, w, field.at[0, :, 1 + (nx - 1) * w], field.at[0, :, (nx + 1) * (1 - w)]),
        lambda w: x_copy(4, w, field.at[1, :, 1 + (nx - 1) * w], field.at[1, :, (nx + 1) * (1 - w)]),
    ]
    y_links = [
        lambda w: y_copy(0, w, bface.at[w], bhalo.at[1 - w]),
        lambda w: y_copy(1, w, sface.at[w], shalo.at[1 - w]),
        lambda w: y_copy(2, w, ysend.at[0, w], yhalo.at[0, 1 - w]),
        lambda w: y_copy(3, w, ysend.at[1, w], yhalo.at[1, 1 - w]),
        lambda w: y_copy(4, w, uface.at[w, pl.ds(0, GROUP)], uhalo.at[1 - w, pl.ds(0, GROUP)]),
        lambda w: y_copy(5, w, uface.at[w, pl.ds(GROUP, GROUP)], uhalo.at[1 - w, pl.ds(GROUP, GROUP)]),
        lambda w: y_copy(6, w, uface.at[w, late], uhalo.at[1 - w, late]),
    ]

    upper = c // (nc // 2)
    other = lax.rem(c + nc // 2, nc)

    def relay_copy(hop, w):
        across = lax.rem(n + step[w] * (1 - upper) + nn, nn)
        if hop == 0:
            src, dst = uface.at[w, late], relay
        else:
            src, dst = relay, uhalo.at[upper * w + (1 - upper) * (1 - w), late]
        return pltpu.make_async_remote_copy(
            src_ref=src, dst_ref=dst, send_sem=relay_send.at[hop], recv_sem=relay_recv.at[hop],
            device_id=(other, across), device_id_type=MESH)

    def relay_receive(hop, w):
        dst = relay if hop == 0 else uhalo.at[w, late]
        pltpu.make_async_remote_copy(
            src_ref=relay, dst_ref=dst, send_sem=relay_send.at[hop], recv_sem=relay_recv.at[hop],
            device_id=(other, n), device_id_type=MESH).wait_recv()

    def send(link, has):
        for w in (0, 1):
            @pl.when(has[w])
            def _():
                link(w).start()

    def receive(link, has):
        for side in (0, 1):
            @pl.when(has[side])
            def _():
                link(1 - side).wait_recv()

    def drain(link, has):
        for w in (0, 1):
            @pl.when(has[w])
            def _():
                link(w).wait_send()

    pick_row = iota((2 * nx, nx * ny), 0)
    from_row = iota((2 * nx, nx * ny), 1)
    wanted = jnp.where(pick_row < nx, pick_row * ny, (pick_row - nx) * ny + ny - 1)
    select[...] = jnp.where(from_row == wanted, 1.0, 0.0).astype(BF16)
    lane_in, lane_out = iota((nz, nz), 0), iota((nz, nz), 1)
    ahead = jnp.where(lane_out == nz - 1, 0, lane_out + 1)
    behind = jnp.where(lane_out == 0, nz - 1, lane_out - 1)
    circ[...] = (jnp.where(lane_in == ahead, 1.0, 0.0) - jnp.where(lane_in == behind, 1.0, 0.0)).astype(BF16)

    def faces_of(block, faces, m):
        for i in range(nv):
            both = dot(select[...], block(m, i).reshape(nx * ny, nz))
            faces[0, m, i] = both[:nx].astype(BF16)
            faces[1, m, i] = both[nx:].astype(BF16)

    for g in range(groups):
        u_load(g).wait()

        def u_mode(m, carry):
            total = jnp.zeros((ny, nz), F32)
            for i in range(nv):
                for x in range(nx):
                    cells = u[m, i, 1 + x].astype(F32)
                    total = total + cells * cells
            total = jnp.sum(total, axis=0, keepdims=True)
            energy[pl.ds(m, 1), :] = total[:, :128] + total[:, 128:]
            faces_of(lambda m, i: u[m, i, pl.ds(1, nx)], uface, m)
            return carry

        lax.fori_loop(g * GROUP, (g + 1) * GROUP, u_mode, 0)
        if g == 0:
            send(y_links[4], far_y)

    def e_copy(index, peer, dst):
        return pltpu.make_async_remote_copy(
            src_ref=energy.at[pl.ds(modes * (0 if index < nc - 1 else 1 if index < nc + zs - 2 else 2), modes)],
            dst_ref=dst, send_sem=es_sem.at[index], recv_sem=er_sem.at[index], device_id=peer, device_id_type=MESH)

    ones = [e_copy(k, first[k], round_one.at[k]) for k in range(nc - 1)]
    twos = [e_copy(nc - 1 + k, second[k], round_two.at[k]) for k in range(zs - 1)]
    threes = [e_copy(nc + zs - 2 + k, third[k], round_three.at[k]) for k in range(rest - 1)]

    def v_faces(g):
        v_load(g).wait()

        def v_mode(m, carry):
            faces_of(lambda m, i: v[m, i], vface, m)
            return carry

        lax.fori_loop(g * GROUP, (g + 1) * GROUP, v_mode, 0, unroll=2)

    def finish(copies, slots, src):
        total = energy[pl.ds(modes * src, modes), :]
        for k, copy in enumerate(copies):
            copy.wait_recv()
            total = total + slots[k]
        return total

    for copy in ones:
        copy.start()
    v_faces(0)
    energy[pl.ds(modes, modes), :] = finish(ones, round_one, 0)
    for copy in twos:
        copy.start()

    mix_load.wait()
    width = 3 * kv
    lane = iota((ny, width), 1)
    row = iota((ny, width), 0)
    lane_row = lax.rem(lane, ny)
    lane_var = lax.rem(lane, kv) // ny
    same = jnp.where(lane_row == row, 1.0, 0.0)
    nxt = jnp.where(lane_row == row + 1, 1.0, 0.0)
    prv = jnp.where(lane_row == row - 1, 1.0, 0.0)
    kinds = ((0, same), (1, nxt - same), (1, same - prv), (2, same), (1, same))
    table = [mix[i] for i in range(nv)]
    for k, (d, stencil) in enumerate(kinds):
        for j in range(nv):
            coefs = jnp.zeros((ny, width), F32)
            for i in range(nv):
                coefs = jnp.where(lane_var == i, table[i][d : d + 1, j : j + 1], coefs)
            mat0[pl.ds((k * nv + j) * ny, ny), :] = coefs * stencil
    high = mat0[...].astype(BF16)
    low = (mat0[...] - high.astype(F32)).astype(BF16)
    mat2[...] = jnp.where(iota(mat0.shape, 1) < 2 * kv, high.astype(F32), low.astype(F32)).astype(BF16)

    v_faces(1)
    energy[pl.ds(2 * modes, modes), :] = finish(twos, round_two, 1)
    for copy in threes:
        copy.start()
    v_faces(2)

    cell_load.wait()
    base_load.wait()
    kind_of = cell[...]
    weight[...] = jnp.where(kind_of == 0, 1.0, jnp.where(kind_of == 1, 0.5, 0.0)).astype(F32)
    for side in (0, 1):
        for x in range(nx):
            bface[side, :, pl.ds(x, 1), :] = base[:, 1 + x, pl.ds((ny - 1) * side, 1), :]

    def base_plane(x, carry):
        for j in range(nv):
            base_dz[j, x] = diff_lanes(base[j, 1 + x])
        return carry

    lax.fori_loop(0, nx, base_plane, 0)
    v_faces(3)

    cells_all = nc * nn * nv * nx * ny * nz
    total = jnp.sum(finish(threes, round_three, 2), axis=1, keepdims=True)
    for w in (0, 1):
        @pl.when(far_y[w])
        def _():
            relay_copy(0, w).start()

    send(y_links[5], far_y)
    send(x_links[0], has_x)
    send(y_links[4], near_y)
    send(y_links[5], near_y)
    send(y_links[6], near_y)
    send(x_links[1], has_x)
    send(y_links[0], has_y)
    amp[...] = jnp.broadcast_to(lax.rsqrt(total / cells_all + 1e-06) / modes, amp.shape)

    def mode_matrix(m, carry):
        scaled = mat0[:, pl.ds(0, 2 * kv)] * amp[pl.ds(m, 1), pl.ds(0, 2 * kv)]
        big = scaled.astype(BF16).astype(F32)
        mats[m] = jnp.where(iota(scaled.shape, 1) < kv, big, scaled - big).astype(BF16)
        return carry

    lax.fori_loop(0, modes, mode_matrix, 0)

    sface[...] = jnp.zeros(sface.shape, F32)
    sx[:, 1] = jnp.zeros((nv, ny, nz), F32)
    sx[:, 2] = jnp.zeros((nv, ny, nz), F32)

    def face_group(g, carry):
        m0 = g * GROUP
        for s in (0, 1):
            x = 1 + (nx - 1) * s
            for k in range(GROUP):
                rows = vface[s, pick[m0 + k]].reshape(kv, nz)
                wface[s, m0 + k] = dot(mats[m0 + k, pl.ds(4 * kv, kv), :], jnp.concatenate([rows, rows], axis=0))
                rows = v[pick[m0 + k], :, x - 1].reshape(kv, nz)
                w_scr[s, k, pl.ds(0, kv), :] = dot(mats[m0 + k, pl.ds(0, kv), :], jnp.concatenate([rows, rows], axis=0))
        for s in (0, 1):
            x = 1 + (nx - 1) * s
            for j in range(nv):
                r = pl.ds(j * ny, ny)
                at_face, at_end = sface[s, j], sx[j, 1 + s]
                for k in range(GROUP):
                    at_face = at_face + wface[s, m0 + k, pl.ds(j * nx, nx), :] * uface[s, m0 + k, j].astype(F32)
                    at_end = at_end + w_scr[s, k, r, :] * u[m0 + k, j, x].astype(F32)
                sface[s, j] = at_face
                sx[j, 1 + s] = at_end
        return carry

    lax.fori_loop(0, groups, face_group, 0)
    send(x_links[2], has_x)
    send(y_links[1], has_y)

    def mix_part(x, g, slot, k):
        m0 = g * MG
        if k == MG:
            du_scr[slot] = dot(u[pl.ds(m0, MG), :, x].reshape(MG * kv, nz), circ[...])
        elif k < MG:
            rows = v[pick[m0 + k], :, x - 1].reshape(kv, nz)
            w_scr[slot, k] = dot(mats[m0 + k, pl.ds(0, 4 * kv), :], jnp.concatenate([rows, rows], axis=0))

    def mix_group(x, g, slot):
        for k in range(MG + 1):
            mix_part(x, g, slot, k)

    def plane_of(t):
        return lax.rem(t + 1, nx) + 1

    def plane(t, carry):
        x = plane_of(t)
        for g in range((modes // MG)):
            slot = g % 2
            for j in range(nv):
                for part in range(j, MG + 1, nv):
                    if g < (modes // MG) - 1:
                        mix_part(x, g + 1, 1 - slot, part)
                    else:
                        mix_part(plane_of(t + 1), 0, 1 - slot, part)
                for h in (0, 1):
                    z = pl.ds(128 * h, 128)
                    if g == 0:
                        q = s_x = s_z = up = down = jnp.zeros((ny, 128), F32)
                    else:
                        q, s_x, s_z, up, down = (acc[i, j, :, z] for i in range(5))
                    for k in range(MG):
                        m = g * MG + k
                        here = u[m, j, x, :, z].astype(F32)
                        dx = u[m, j, x + 1, :, z].astype(F32) - u[m, j, x - 1, :, z].astype(F32)
                        dz = du_scr[slot, pl.ds(k * kv + j * ny, ny), z]
                        wx, wp, wm, wz = (w_scr[slot, k, pl.ds(i * kv + j * ny, ny), z] for i in range(4))
                        q = q + dx * wx + dz * wz
                        s_x = s_x + here * wx
                        s_z = s_z + here * wz
                        up = up + here * wm
                        down = down + here * wp
                    for i, value in enumerate((q, s_x, s_z, up, down)):
                        acc[i, j, :, z] = value
                if g == (modes // MG) - 1:
                    grad[j, x - 1] = acc[0, j] - diff_lanes(acc[2, j]) - rows_up(acc[3, j]) - rows_down(acc[4, j])
                    sx_all[j, x - 1] = acc[1, j]
        return carry

    mix_group(plane_of(0), 0, 0)
    lax.fori_loop(0, nx // 2, plane, 0)
    for w in (0, 1):
        @pl.when(far_y[w])
        def _():
            relay_receive(0, w)
            relay_copy(1, w).start()

    lax.fori_loop(nx // 2, nx - 2, plane, 0)
    receive(x_links[0], has_x)
    lax.fori_loop(nx - 2, nx, plane, 0)

    receive(y_links[4], has_y)
    receive(y_links[5], has_y)
    receive(y_links[6], near_y)
    for w in (0, 1):
        @pl.when(far_y[w])
        def _():
            relay_receive(1, w)

    fterm[...] = jnp.zeros(fterm.shape, F32)

    def cross_mode(m, carry):
        for s in (0, 1):
            fterm[s] += wface[s, m].reshape(nv, nx, nz) * uhalo[s, m].astype(F32)
        return carry

    lax.fori_loop(0, modes, cross_mode, 0)
    receive(y_links[1], has_y)
    receive(x_links[2], has_x)
    fterm[0] = shalo[0] - fterm[0]
    fterm[1] = fterm[1] - shalo[1]

    def add_rows(target, x0):
        for side in (0, 1):
            for x in range(nx):
                end = pl.ds((ny - 1) * side, 1)
                target[:, x + x0, end, :] = target[:, x + x0, end, :] + fterm[side, :, pl.ds(x, 1), :]

    def grad_plane(x, carry):
        for j in range(nv):
            grad[j, x] = grad[j, x] - (sx_all[j, x + 1] - sx_all[j, x - 1])
        return carry

    for j in range(nv):
        grad[j, 0] = grad[j, 0] - (sx_all[j, 1] - sx[j, 0])
        grad[j, nx - 1] = grad[j, nx - 1] - (sx[j, 3] - sx_all[j, nx - 2])
    lax.fori_loop(1, nx - 1, grad_plane, 0, unroll=2)
    add_rows(grad, 0)

    def apply(slot, source, target):
        def weigh(x, carry):
            for j in range(nv):
                field[slot, j, x + 1] = weight[x] * source[j, x]
            return carry

        lax.fori_loop(0, nx, weigh, 0, unroll=2)
        for side in (0, 1):
            for x in range(nx):
                ysend[slot, side, :, pl.ds(x, 1), :] = field[slot, :, 1 + x, pl.ds((ny - 1) * side, 1), :]
        send(x_links[3 + slot], has_x)
        send(y_links[2 + slot], has_y)


        def mixed(x, carry):
            wall[x] = dot(mat2[pl.ds(0, 4 * kv), :], split3(field[slot, :, x].reshape(kv, nz)))
            return carry

        lax.fori_loop(1, nx + 1, mixed, 0, unroll=4)
        own = [dot(mat2[pl.ds(4 * kv, kv), :], split3(ysend[slot, s].reshape(kv, nz))) for s in (0, 1)]
        for s in (0, 1):
            wface[s, 0] = own[s]

        def result_plane(x, carry):
            for j in range(nv):
                r = pl.ds(j * ny, ny)
                wx = wall[x, r, :]
                wp, wm, wz = (wall[x, pl.ds(t * kv + j * ny, ny), :] for t in (1, 2, 3))
                here = base[j, x]
                value = base[j, x + 1] * (wx - wall[x + 1, r, :]) - base[j, x - 1] * (wx - wall[x - 1, r, :])
                value = value + base_dz[j, x - 1] * wz - diff_lanes(here * wz)
                target[j, x - 1] = value - rows_up(here * wm) - rows_down(here * wp)
            return carry

        lax.fori_loop(2, nx, result_plane, 0, unroll=2)
        if slot == 0:
            receive(x_links[1], has_x)
            receive(y_links[0], has_y)
        receive(x_links[3 + slot], has_x)
        receive(y_links[2 + slot], has_y)
        for x in (0, nx + 1):
            wall[x, pl.ds(0, kv), :] = dot(mat2[pl.ds(0, kv), :], split3(field[slot, :, x].reshape(kv, nz)))
        lax.fori_loop(0, 2, lambda s, carry: result_plane(1 + (nx - 1) * s, carry), 0, unroll=2)
        for s in (0, 1):
            far = dot(mat2[pl.ds(4 * kv, kv), :], split3(yhalo[slot, s].reshape(kv, nz)))
            change = (far - wface[s, 0]).reshape(nv, nx, nz) * bhalo[s]
            fterm[s] = change if s == 0 else -change
        add_rows(target, 0)

    apply(0, grad, result)
    apply(1, result, grad)
    store = pltpu.make_async_copy(grad, out_hbm, out_sem)
    store.start()
    for link in x_links:
        drain(link, has_x)
    for link in y_links[:6]:
        drain(link, has_y)
    drain(y_links[6], near_y)
    for w in (0, 1):
        @pl.when(far_y[w])
        def _():
            relay_copy(0, w).wait_send()
            relay_copy(1, w).wait_send()

    for copy in ones + twos + threes:
        copy.wait_send()
    store.wait()


def per_device(u, v, base, cell, pick, mix, *, interpret=False):
    modes, nv, nx, ny, nz = u.shape
    nc, nn = lax.axis_size("chord"), lax.axis_size("normal")
    kv = nv * ny
    groups = modes // GROUP
    vm = pltpu.VMEM
    any_space = pl.BlockSpec(memory_space=pl.ANY)
    smem = pl.BlockSpec(memory_space=pltpu.SMEM)
    return pl.pallas_call(
        functools.partial(kernel, (nc, nn, modes, nv, nx, ny, nz)),
        out_shape=jax.ShapeDtypeStruct(base.shape, F32),
        in_specs=[any_space] * 5 + [smem],
        out_specs=any_space,
        scratch_shapes=[
            vm((modes, nv, nx + 2, ny, nz), BF16),
            vm((modes, nv, nx, ny, nz), BF16),
            vm((nv, nx + 2, ny, nz), F32),
            vm((nx, ny, nz), jnp.int32),
            vm((nv, 3, nv), F32),
            vm((2, modes, nv, nx, nz), BF16),
            vm((2, modes, nv, nx, nz), BF16),
            vm((2, modes, nv, nx, nz), BF16),
            vm((2, modes, kv, nz), F32),
            vm((modes, 5 * kv, 2 * kv), BF16),
            vm((5 * kv, 3 * kv), BF16),
            vm((5 * kv, 3 * kv), F32),
            vm((2 * nx, nx * ny), BF16),
            vm((nz, nz), BF16),
            vm((2, max(GROUP, MG), 4 * kv, nz), F32),
            vm((2, MG * kv, nz), F32),
            vm((5, nv, ny, nz), F32),
            vm((nv, nx, ny, nz), F32),
            vm((nv, 4, ny, nz), F32),
            vm((nv, nx, ny, nz), F32),
            vm((2, nv, nx, nz), F32),
            vm((2, nv, nx, nz), F32),
            vm((2, 2, nv, nx, nz), F32),
            vm((2, 2, nv, nx, nz), F32),
            vm((2, nv, nx + 2, ny, nz), F32),
            vm((nx + 2, 4 * kv, nz), F32),
            vm((nv, nx, ny, nz), F32),
            vm((2, nv, nx, nz), F32),
            vm((2, nv, nx, nz), F32),
            vm((2, nv, nx, nz), F32),
            vm((modes - 2 * GROUP, nv, nx, nz), BF16),
            vm((3 * modes, 128), F32),
            vm((nc - 1, modes, 128), F32),
            vm((3, modes, 128), F32),
            vm((max(nn // 4 - 1, 1), modes, 128), F32),
            vm((modes, 256), F32),
            vm((nx, ny, nz), F32),
            vm((nv, nx, ny, nz), F32),
            pltpu.SemaphoreType.DMA((2 * groups + 3,)),
            pltpu.SemaphoreType.DMA((5, 2)),
            pltpu.SemaphoreType.DMA((5, 2)),
            pltpu.SemaphoreType.DMA((7, 2)),
            pltpu.SemaphoreType.DMA((7, 2)),
            pltpu.SemaphoreType.DMA((2,)),
            pltpu.SemaphoreType.DMA((2,)),
            pltpu.SemaphoreType.DMA((nc + nn // 4 + 1,)),
            pltpu.SemaphoreType.DMA((nc + nn // 4 + 1,)),
            pltpu.SemaphoreType.DMA,
        ],
        compiler_params=pltpu.CompilerParams(
            collective_id=0, has_side_effects=True, vmem_limit_bytes=60 * 2**20),
    )(u, v, base, cell, mix.transpose(1, 0, 2), pick)


def solution(mesh):
    return jax.shard_map(
        per_device,
        mesh=mesh,
        in_specs=(
            P(None, None, "chord", "normal", None),
            P(None, None, "chord", "normal", None),
            P(None, "chord", "normal", None),
            P("chord", "normal", None),
            P(),
            P(),
        ),
        out_specs=P(None, "chord", "normal", None),
        check_vma=False,
    )
```

```python
import functools

import jax
import jax.numpy as jnp
from jax import lax
from jax.experimental import pallas as pl
from jax.experimental.pallas import tpu as pltpu
from jax.sharding import PartitionSpec as P

MESH = pl.DeviceIdType.MESH
F32 = jnp.float32
BF16 = jnp.bfloat16
GROUP = 4
MG = 2


def iota(shape, dim):
    return lax.broadcasted_iota(jnp.int32, shape, dim)


def diff_lanes(x):
    lanes = x.shape[-1]
    return pltpu.roll(x, lanes - 1, 1) - pltpu.roll(x, 1, 1)


def rows_up(x):
    rows = x.shape[0]
    return jnp.where(iota(x.shape, 0) == rows - 1, 0.0, pltpu.roll(x, rows - 1, 0))


def rows_down(x):
    return jnp.where(iota(x.shape, 0) == 0, 0.0, pltpu.roll(x, 1, 0))


def split3(x):
    high = x.astype(BF16)
    low = (x - high.astype(F32)).astype(BF16)
    return jnp.concatenate([high, low, high], axis=0)


def dot(a, b):
    return jnp.dot(a, b, preferred_element_type=F32)


def kernel(
    sizes,
    u_hbm, v_hbm, base_hbm, cell_hbm, mix_hbm, pick,
    out_hbm,
    u, v, base, cell, mix, uface, vface, uhalo, wface, mats, mat2, mat0, select, circ,
    w_scr, du_scr, acc, grad, sx, sx_all, sface, shalo, ysend, yhalo, field, wall, base_dz, bface, bhalo,
    fterm, energy, round_one, round_two, round_three, amp, weight,
    load_sem, xs_sem, xr_sem, ys_sem, yr_sem, es_sem, er_sem, out_sem,
):
    nc, nn, modes, nv, nx, ny, nz = sizes
    kv = nv * ny
    c, n = lax.axis_index("chord"), lax.axis_index("normal")
    has_x = (c > 0, c < nc - 1)
    has_y = (n > 0, n < nn - 1)
    half = nn // 2
    far_y = (n == half, n == half - 1)
    far = jnp.logical_or(*far_y)
    far_x = tuple(jnp.logical_and(a, far) for a in has_x)
    near_x = tuple(jnp.logical_and(a, jnp.logical_not(far)) for a in has_x)
    near_y = tuple(jnp.logical_and(a, jnp.logical_not(b)) for a, b in zip(has_y, far_y))
    step = (-1, 1)
    zs, rest = 4, nn // 4
    groups = modes // GROUP

    def u_load(g):
        s = pl.ds(g * GROUP, GROUP)
        return pltpu.make_async_copy(u_hbm.at[s], u.at[s, :, pl.ds(1, nx)], load_sem.at[g])

    def v_load(g):
        s = pl.ds(g * GROUP, GROUP)
        return pltpu.make_async_copy(v_hbm.at[s], v.at[s], load_sem.at[groups + g])

    base_load = pltpu.make_async_copy(base_hbm, base.at[:, pl.ds(1, nx)], load_sem.at[2 * groups])
    cell_load = pltpu.make_async_copy(cell_hbm, cell, load_sem.at[2 * groups + 1])
    mix_load = pltpu.make_async_copy(mix_hbm, mix, load_sem.at[2 * groups + 2])
    mix_load.start()
    for g in range(groups):
        u_load(g).start()
    base_load.start()
    cell_load.start()
    for g in range(groups):
        v_load(g).start()

    first = [(lax.rem(c + k, nc), n) for k in range(1, nc)]
    second = [(c, n // zs * zs + lax.rem(lax.rem(n, zs) + k, zs)) for k in range(1, zs)]
    third = [(c, lax.rem(n // zs + k, rest) * zs + lax.rem(n, zs)) for k in range(1, rest)]
    around = [(c, lax.rem(n + 1, nn)), (c, lax.rem(n + nn - 1, nn))]
    barrier = pltpu.get_barrier_semaphore()
    peers = first + second + third + around
    for peer in peers:
        pl.semaphore_signal(barrier, inc=1, device_id=peer, device_id_type=MESH)

    @pl.when(c == 0)
    def _():
        u[:, :, 0] = jnp.zeros((modes, nv, ny, nz), BF16)
        base[:, 0] = jnp.zeros((nv, ny, nz), F32)
        sx[:, 0] = jnp.zeros((nv, ny, nz), F32)
        field[0, :, 0] = jnp.zeros((nv, ny, nz), F32)
        field[1, :, 0] = jnp.zeros((nv, ny, nz), F32)

    @pl.when(c == nc - 1)
    def _():
        u[:, :, nx + 1] = jnp.zeros((modes, nv, ny, nz), BF16)
        base[:, nx + 1] = jnp.zeros((nv, ny, nz), F32)
        sx[:, 3] = jnp.zeros((nv, ny, nz), F32)
        field[0, :, nx + 1] = jnp.zeros((nv, ny, nz), F32)
        field[1, :, nx + 1] = jnp.zeros((nv, ny, nz), F32)

    for side, at_edge in ((0, n == 0), (1, n == nn - 1)):
        @pl.when(at_edge)
        def _():
            uhalo[side] = jnp.zeros((modes, nv, nx, nz), BF16)
            bhalo[side] = jnp.zeros((nv, nx, nz), F32)
            shalo[side] = jnp.zeros((nv, nx, nz), F32)
            yhalo[0, side] = jnp.zeros((nv, nx, nz), F32)
            yhalo[1, side] = jnp.zeros((nv, nx, nz), F32)

    pl.semaphore_wait(barrier, len(peers))

    def x_copy(kind, way, src, dst):
        return pltpu.make_async_remote_copy(
            src_ref=src, dst_ref=dst, send_sem=xs_sem.at[kind, way], recv_sem=xr_sem.at[kind, 1 - way],
            device_id=(lax.rem(c + step[way] + nc, nc), n), device_id_type=MESH)

    def y_copy(kind, way, src, dst):
        return pltpu.make_async_remote_copy(
            src_ref=src, dst_ref=dst, send_sem=ys_sem.at[kind, way], recv_sem=yr_sem.at[kind, 1 - way],
            device_id=(c, lax.rem(n + step[way] + nn, nn)), device_id_type=MESH)

    front, back = pl.ds(0, modes // 2), pl.ds(modes // 2, modes // 2)
    x_links = [
        lambda w: x_copy(0, w, u_hbm.at[front, :, (nx - 1) * w], u.at[front, :, (nx + 1) * (1 - w)]),
        lambda w: x_copy(1, w, base_hbm.at[:, (nx - 1) * w], base.at[:, (nx + 1) * (1 - w)]),
        lambda w: x_copy(2, w, sx.at[:, 1 + w], sx.at[:, 3 * (1 - w)]),
        lambda w: x_copy(3, w, field.at[0, :, 1 + (nx - 1) * w], field.at[0, :, (nx + 1) * (1 - w)]),
        lambda w: x_copy(4, w, field.at[1, :, 1 + (nx - 1) * w], field.at[1, :, (nx + 1) * (1 - w)]),
        lambda w: x_copy(5, w, u_hbm.at[back, :, (nx - 1) * w], u.at[back, :, (nx + 1) * (1 - w)]),
    ]
    y_links = [
        lambda w: y_copy(0, w, bface.at[w], bhalo.at[1 - w]),
        lambda w: y_copy(1, w, sface.at[w], shalo.at[1 - w]),
        lambda w: y_copy(2, w, ysend.at[0, w], yhalo.at[0, 1 - w]),
        lambda w: y_copy(3, w, ysend.at[1, w], yhalo.at[1, 1 - w]),
        lambda w: y_copy(4, w, uface.at[w, pl.ds(0, GROUP)], uhalo.at[1 - w, pl.ds(0, GROUP)]),
        lambda w: y_copy(5, w, uface.at[w, pl.ds(GROUP, modes - GROUP)], uhalo.at[1 - w, pl.ds(GROUP, modes - GROUP)]),
    ]

    def send(link, has):
        for w in (0, 1):
            @pl.when(has[w])
            def _():
                link(w).start()

    def receive(link, has):
        for side in (0, 1):
            @pl.when(has[side])
            def _():
                link(1 - side).wait_recv()

    def drain(link, has):
        for w in (0, 1):
            @pl.when(has[w])
            def _():
                link(w).wait_send()

    send(x_links[0], far_x)

    pick_row = iota((2 * nx, nx * ny), 0)
    from_row = iota((2 * nx, nx * ny), 1)
    wanted = jnp.where(pick_row < nx, pick_row * ny, (pick_row - nx) * ny + ny - 1)
    select[...] = jnp.where(from_row == wanted, 1.0, 0.0).astype(BF16)
    lane_in, lane_out = iota((nz, nz), 0), iota((nz, nz), 1)
    ahead = jnp.where(lane_out == nz - 1, 0, lane_out + 1)
    behind = jnp.where(lane_out == 0, nz - 1, lane_out - 1)
    circ[...] = (jnp.where(lane_in == ahead, 1.0, 0.0) - jnp.where(lane_in == behind, 1.0, 0.0)).astype(BF16)

    def faces_of(block, faces, m):
        for i in range(nv):
            both = dot(select[...], block(m, i).reshape(nx * ny, nz))
            faces[0, m, i] = both[:nx].astype(BF16)
            faces[1, m, i] = both[nx:].astype(BF16)

    for g in range(groups):
        u_load(g).wait()

        def u_mode(m, carry):
            total = jnp.zeros((ny, nz), F32)
            for i in range(nv):
                for x in range(nx):
                    cells = u[m, i, 1 + x].astype(F32)
                    total = total + cells * cells
            total = jnp.sum(total, axis=0, keepdims=True)
            energy[pl.ds(m, 1), :] = total[:, :128] + total[:, 128:]
            faces_of(lambda m, i: u[m, i, pl.ds(1, nx)], uface, m)
            return carry

        lax.fori_loop(g * GROUP, (g + 1) * GROUP, u_mode, 0)
        if g == 0:
            send(y_links[4], far_y)

    def e_copy(index, peer, dst):
        return pltpu.make_async_remote_copy(
            src_ref=energy.at[pl.ds(modes * (0 if index < nc - 1 else 1 if index < nc + zs - 2 else 2), modes)],
            dst_ref=dst, send_sem=es_sem.at[index], recv_sem=er_sem.at[index], device_id=peer, device_id_type=MESH)

    ones = [e_copy(k, first[k], round_one.at[k]) for k in range(nc - 1)]
    twos = [e_copy(nc - 1 + k, second[k], round_two.at[k]) for k in range(zs - 1)]
    threes = [e_copy(nc + zs - 2 + k, third[k], round_three.at[k]) for k in range(rest - 1)]

    def v_faces(g):
        v_load(g).wait()

        def v_mode(m, carry):
            faces_of(lambda m, i: v[m, i], vface, m)
            return carry

        lax.fori_loop(g * GROUP, (g + 1) * GROUP, v_mode, 0, unroll=2)

    def finish(copies, slots, src):
        total = energy[pl.ds(modes * src, modes), :]
        for k, copy in enumerate(copies):
            copy.wait_recv()
            total = total + slots[k]
        return total

    for copy in ones:
        copy.start()
    v_faces(0)
    energy[pl.ds(modes, modes), :] = finish(ones, round_one, 0)
    for copy in twos:
        copy.start()

    mix_load.wait()
    width = 3 * kv
    lane = iota((ny, width), 1)
    row = iota((ny, width), 0)
    lane_row = lax.rem(lane, ny)
    lane_var = lax.rem(lane, kv) // ny
    same = jnp.where(lane_row == row, 1.0, 0.0)
    nxt = jnp.where(lane_row == row + 1, 1.0, 0.0)
    prv = jnp.where(lane_row == row - 1, 1.0, 0.0)
    kinds = ((0, same), (1, nxt - same), (1, same - prv), (2, same), (1, same))
    table = [mix[i] for i in range(nv)]
    for k, (d, stencil) in enumerate(kinds):
        for j in range(nv):
            coefs = jnp.zeros((ny, width), F32)
            for i in range(nv):
                coefs = jnp.where(lane_var == i, table[i][d : d + 1, j : j + 1], coefs)
            mat0[pl.ds((k * nv + j) * ny, ny), :] = coefs * stencil
    high = mat0[...].astype(BF16)
    low = (mat0[...] - high.astype(F32)).astype(BF16)
    mat2[...] = jnp.where(iota(mat0.shape, 1) < 2 * kv, high.astype(F32), low.astype(F32)).astype(BF16)

    v_faces(1)
    energy[pl.ds(2 * modes, modes), :] = finish(twos, round_two, 1)
    for copy in threes:
        copy.start()
    v_faces(2)

    cell_load.wait()
    base_load.wait()
    kind_of = cell[...]
    weight[...] = jnp.where(kind_of == 0, 1.0, jnp.where(kind_of == 1, 0.5, 0.0)).astype(F32)
    for side in (0, 1):
        for x in range(nx):
            bface[side, :, pl.ds(x, 1), :] = base[:, 1 + x, pl.ds((ny - 1) * side, 1), :]

    def base_plane(x, carry):
        for j in range(nv):
            base_dz[j, x] = diff_lanes(base[j, 1 + x])
        return carry

    lax.fori_loop(0, nx, base_plane, 0)
    v_faces(3)

    cells_all = nc * nn * nv * nx * ny * nz
    total = jnp.sum(finish(threes, round_three, 2), axis=1, keepdims=True)
    send(y_links[5], far_y)
    send(x_links[0], near_x)
    send(x_links[5], has_x)
    send(y_links[4], near_y)
    send(y_links[5], near_y)
    send(x_links[1], has_x)
    send(y_links[0], has_y)
    amp[...] = jnp.broadcast_to(lax.rsqrt(total / cells_all + 1e-06) / modes, amp.shape)

    def mode_matrix(m, carry):
        scaled = mat0[:, pl.ds(0, 2 * kv)] * amp[pl.ds(m, 1), pl.ds(0, 2 * kv)]
        big = scaled.astype(BF16).astype(F32)
        mats[m] = jnp.where(iota(scaled.shape, 1) < kv, big, scaled - big).astype(BF16)
        return carry

    lax.fori_loop(0, modes, mode_matrix, 0)

    sface[...] = jnp.zeros(sface.shape, F32)
    sx[:, 1] = jnp.zeros((nv, ny, nz), F32)
    sx[:, 2] = jnp.zeros((nv, ny, nz), F32)

    def face_group(g, carry):
        m0 = g * GROUP
        for s in (0, 1):
            x = 1 + (nx - 1) * s
            for k in range(GROUP):
                rows = vface[s, pick[m0 + k]].reshape(kv, nz)
                wface[s, m0 + k] = dot(mats[m0 + k, pl.ds(4 * kv, kv), :], jnp.concatenate([rows, rows], axis=0))
                rows = v[pick[m0 + k], :, x - 1].reshape(kv, nz)
                w_scr[s, k, pl.ds(0, kv), :] = dot(mats[m0 + k, pl.ds(0, kv), :], jnp.concatenate([rows, rows], axis=0))
        for s in (0, 1):
            x = 1 + (nx - 1) * s
            for j in range(nv):
                r = pl.ds(j * ny, ny)
                at_face, at_end = sface[s, j], sx[j, 1 + s]
                for k in range(GROUP):
                    at_face = at_face + wface[s, m0 + k, pl.ds(j * nx, nx), :] * uface[s, m0 + k, j].astype(F32)
                    at_end = at_end + w_scr[s, k, r, :] * u[m0 + k, j, x].astype(F32)
                sface[s, j] = at_face
                sx[j, 1 + s] = at_end
        return carry

    lax.fori_loop(0, groups, face_group, 0)
    send(x_links[2], has_x)
    send(y_links[1], has_y)

    def mix_part(x, g, slot, k):
        m0 = g * MG
        if k == MG:
            du_scr[slot] = dot(u[pl.ds(m0, MG), :, x].reshape(MG * kv, nz), circ[...])
        elif k < MG:
            rows = v[pick[m0 + k], :, x - 1].reshape(kv, nz)
            w_scr[slot, k] = dot(mats[m0 + k, pl.ds(0, 4 * kv), :], jnp.concatenate([rows, rows], axis=0))

    def mix_group(x, g, slot):
        for k in range(MG + 1):
            mix_part(x, g, slot, k)

    def plane_of(t):
        return lax.rem(t + 1, nx) + 1

    def plane(t, carry):
        x = plane_of(t)
        for g in range((modes // MG)):
            slot = g % 2
            for j in range(nv):
                for part in range(j, MG + 1, nv):
                    if g < (modes // MG) - 1:
                        mix_part(x, g + 1, 1 - slot, part)
                    else:
                        mix_part(plane_of(t + 1), 0, 1 - slot, part)
                for h in (0, 1):
                    z = pl.ds(128 * h, 128)
                    if g == 0:
                        q = s_x = s_z = up = down = jnp.zeros((ny, 128), F32)
                    else:
                        q, s_x, s_z, up, down = (acc[i, j, :, z] for i in range(5))
                    for k in range(MG):
                        m = g * MG + k
                        here = u[m, j, x, :, z].astype(F32)
                        dx = u[m, j, x + 1, :, z].astype(F32) - u[m, j, x - 1, :, z].astype(F32)
                        dz = du_scr[slot, pl.ds(k * kv + j * ny, ny), z]
                        wx, wp, wm, wz = (w_scr[slot, k, pl.ds(i * kv + j * ny, ny), z] for i in range(4))
                        q = q + dx * wx + dz * wz
                        s_x = s_x + here * wx
                        s_z = s_z + here * wz
                        up = up + here * wm
                        down = down + here * wp
                    for i, value in enumerate((q, s_x, s_z, up, down)):
                        acc[i, j, :, z] = value
                if g == (modes // MG) - 1:
                    grad[j, x - 1] = acc[0, j] - diff_lanes(acc[2, j]) - rows_up(acc[3, j]) - rows_down(acc[4, j])
                    sx_all[j, x - 1] = acc[1, j]
        return carry

    mix_group(plane_of(0), 0, 0)
    lax.fori_loop(0, nx - 2, plane, 0)
    receive(x_links[0], has_x)
    receive(x_links[5], has_x)
    lax.fori_loop(nx - 2, nx, plane, 0)

    receive(x_links[2], has_x)
    for j in range(nv):
        field[0, j, 1] = weight[0] * (grad[j, 0] - (sx_all[j, 1] - sx[j, 0]))
        field[0, j, nx] = weight[nx - 1] * (grad[j, nx - 1] - (sx[j, 3] - sx_all[j, nx - 2]))

    def grad_plane(x, carry):
        for j in range(nv):
            field[0, j, x + 1] = weight[x] * (grad[j, x] - (sx_all[j, x + 1] - sx_all[j, x - 1]))
        return carry

    lax.fori_loop(1, nx - 1, grad_plane, 0, unroll=2)
    receive(y_links[4], has_y)
    receive(y_links[1], has_y)

    def cross(first_mode, last_mode):
        def terms(j, carry):
            for s in (0, 1):
                value = (shalo if first_mode == 0 else fterm)[s, j]
                value = -value if first_mode == 0 and s == 1 else value
                for m in range(first_mode, last_mode):
                    term = wface[s, m, pl.ds(pl.multiple_of(j * nx, nx), nx), :] * uhalo[s, m, j].astype(F32)
                    value = value - term if s == 0 else value + term
                fterm[s, j] = value
            return carry

        lax.fori_loop(0, nv, terms, 0)

    cross(0, GROUP)
    receive(y_links[5], has_y)
    cross(GROUP, modes)

    def add_rows(target, x0, weighted):
        for side in (0, 1):
            end = pl.ds((ny - 1) * side, 1)
            for x in range(nx):
                change = fterm[side, :, pl.ds(x, 1), :]
                if weighted:
                    change = change * weight[x, end, :]
                target[:, x + x0, end, :] = target[:, x + x0, end, :] + change

    add_rows(field.at[0], 1, True)

    def apply(slot):
        target = field.at[1] if slot == 0 else grad
        shift = 0 if slot == 0 else 1
        for side in (0, 1):
            for x in range(nx):
                ysend[slot, side, :, pl.ds(x, 1), :] = field[slot, :, 1 + x, pl.ds((ny - 1) * side, 1), :]
        send(y_links[2 + slot], has_y)
        send(x_links[3 + slot], has_x)

        def mixed(x, carry):
            wall[x] = dot(mat2[pl.ds(0, 4 * kv), :], split3(field[slot, :, x].reshape(kv, nz)))
            return carry

        lax.fori_loop(1, nx + 1, mixed, 0, unroll=4)
        for s in (0, 1):
            wface[s, 0] = dot(mat2[pl.ds(4 * kv, kv), :], split3(ysend[slot, s].reshape(kv, nz)))

        def result_plane(x, carry):
            for j in range(nv):
                r = pl.ds(j * ny, ny)
                wx = wall[x, r, :]
                wp, wm, wz = (wall[x, pl.ds(t * kv + j * ny, ny), :] for t in (1, 2, 3))
                here = base[j, x]
                value = base[j, x + 1] * (wx - wall[x + 1, r, :]) - base[j, x - 1] * (wx - wall[x - 1, r, :])
                value = value + base_dz[j, x - 1] * wz - diff_lanes(here * wz)
                value = value - rows_up(here * wm) - rows_down(here * wp)
                target[j, x - shift] = weight[x - 1] * value if slot == 0 else value
            return carry

        lax.fori_loop(2, nx, result_plane, 0, unroll=2)
        if slot == 0:
            receive(x_links[1], has_x)
            receive(y_links[0], has_y)
        receive(y_links[2 + slot], has_y)
        for s in (0, 1):
            far_side = dot(mat2[pl.ds(4 * kv, kv), :], split3(yhalo[slot, s].reshape(kv, nz)))
            change = (far_side - wface[s, 0]).reshape(nv, nx, nz) * bhalo[s]
            fterm[s] = change if s == 0 else -change
        receive(x_links[3 + slot], has_x)
        for x in (0, nx + 1):
            wall[x, pl.ds(0, kv), :] = dot(mat2[pl.ds(0, kv), :], split3(field[slot, :, x].reshape(kv, nz)))
        lax.fori_loop(0, 2, lambda s, carry: result_plane(1 + (nx - 1) * s, carry), 0, unroll=2)
        add_rows(target, 1 - shift, slot == 0)

    apply(0)
    apply(1)
    store = pltpu.make_async_copy(grad, out_hbm, out_sem)
    store.start()
    for link in x_links:
        drain(link, has_x)
    for link in y_links:
        drain(link, has_y)
    for copy in ones + twos + threes:
        copy.wait_send()
    store.wait()


def per_device(u, v, base, cell, pick, mix, *, interpret=False):
    modes, nv, nx, ny, nz = u.shape
    nc, nn = lax.axis_size("chord"), lax.axis_size("normal")
    kv = nv * ny
    groups = modes // GROUP
    vm = pltpu.VMEM
    any_space = pl.BlockSpec(memory_space=pl.ANY)
    smem = pl.BlockSpec(memory_space=pltpu.SMEM)
    return pl.pallas_call(
        functools.partial(kernel, (nc, nn, modes, nv, nx, ny, nz)),
        out_shape=jax.ShapeDtypeStruct(base.shape, F32),
        in_specs=[any_space] * 5 + [smem],
        out_specs=any_space,
        scratch_shapes=[
            vm((modes, nv, nx + 2, ny, nz), BF16),
            vm((modes, nv, nx, ny, nz), BF16),
            vm((nv, nx + 2, ny, nz), F32),
            vm((nx, ny, nz), jnp.int32),
            vm((nv, 3, nv), F32),
            vm((2, modes, nv, nx, nz), BF16),
            vm((2, modes, nv, nx, nz), BF16),
            vm((2, modes, nv, nx, nz), BF16),
            vm((2, modes, kv, nz), F32),
            vm((modes, 5 * kv, 2 * kv), BF16),
            vm((5 * kv, 3 * kv), BF16),
            vm((5 * kv, 3 * kv), F32),
            vm((2 * nx, nx * ny), BF16),
            vm((nz, nz), BF16),
            vm((2, max(GROUP, MG), 4 * kv, nz), F32),
            vm((2, MG * kv, nz), F32),
            vm((5, nv, ny, nz), F32),
            vm((nv, nx, ny, nz), F32),
            vm((nv, 4, ny, nz), F32),
            vm((nv, nx, ny, nz), F32),
            vm((2, nv, nx, nz), F32),
            vm((2, nv, nx, nz), F32),
            vm((2, 2, nv, nx, nz), F32),
            vm((2, 2, nv, nx, nz), F32),
            vm((2, nv, nx + 2, ny, nz), F32),
            vm((nx + 2, 4 * kv, nz), F32),
            vm((nv, nx, ny, nz), F32),
            vm((2, nv, nx, nz), F32),
            vm((2, nv, nx, nz), F32),
            vm((2, nv, nx, nz), F32),
            vm((3 * modes, 128), F32),
            vm((nc - 1, modes, 128), F32),
            vm((3, modes, 128), F32),
            vm((max(nn // 4 - 1, 1), modes, 128), F32),
            vm((modes, 256), F32),
            vm((nx, ny, nz), F32),
            pltpu.SemaphoreType.DMA((2 * groups + 3,)),
            pltpu.SemaphoreType.DMA((6, 2)),
            pltpu.SemaphoreType.DMA((6, 2)),
            pltpu.SemaphoreType.DMA((6, 2)),
            pltpu.SemaphoreType.DMA((6, 2)),
            pltpu.SemaphoreType.DMA((nc + nn // 4 + 1,)),
            pltpu.SemaphoreType.DMA((nc + nn // 4 + 1,)),
            pltpu.SemaphoreType.DMA,
        ],
        compiler_params=pltpu.CompilerParams(
            collective_id=0, has_side_effects=True, vmem_limit_bytes=60 * 2**20),
    )(u, v, base, cell, mix.transpose(1, 0, 2), pick)


def solution(mesh):
    return jax.shard_map(
        per_device,
        mesh=mesh,
        in_specs=(
            P(None, None, "chord", "normal", None),
            P(None, None, "chord", "normal", None),
            P(None, "chord", "normal", None),
            P("chord", "normal", None),
            P(),
            P(),
        ),
        out_specs=P(None, "chord", "normal", None),
        check_vma=False,
    )
```

```python
import functools

import jax
import jax.numpy as jnp
from jax import lax
from jax.experimental import pallas as pl
from jax.experimental.pallas import tpu as pltpu
from jax.sharding import PartitionSpec as P

MESH = pl.DeviceIdType.MESH
F32 = jnp.float32
BF16 = jnp.bfloat16
GROUP = 4
MG = 2


def iota(shape, dim):
    return lax.broadcasted_iota(jnp.int32, shape, dim)


def diff_lanes(x):
    lanes = x.shape[-1]
    return pltpu.roll(x, lanes - 1, 1) - pltpu.roll(x, 1, 1)


def rows_up(x):
    rows = x.shape[0]
    return jnp.where(iota(x.shape, 0) == rows - 1, 0.0, pltpu.roll(x, rows - 1, 0))


def rows_down(x):
    return jnp.where(iota(x.shape, 0) == 0, 0.0, pltpu.roll(x, 1, 0))


def split3(x):
    high = x.astype(BF16)
    low = (x - high.astype(F32)).astype(BF16)
    return jnp.concatenate([high, low, high], axis=0)


def dot(a, b):
    return jnp.dot(a, b, preferred_element_type=F32)


def kernel(
    sizes,
    u_hbm, v_hbm, base_hbm, cell_hbm, mix_hbm, pick,
    out_hbm,
    u, v, base, cell, mix, uface, vface, uhalo, wface, mats, mat2, mat0, select, circ,
    w_scr, du_scr, acc, grad, sx, sx_all, sface, shalo, ysend, yhalo, field, wall, base_dz, bface, bhalo,
    fterm, energy, round_one, round_two, round_three, amp, weight,
    load_sem, xs_sem, xr_sem, ys_sem, yr_sem, es_sem, er_sem, out_sem,
):
    nc, nn, modes, nv, nx, ny, nz = sizes
    kv = nv * ny
    c, n = lax.axis_index("chord"), lax.axis_index("normal")
    has_x = (c > 0, c < nc - 1)
    has_y = (n > 0, n < nn - 1)
    half = nn // 2
    far_y = (n == half, n == half - 1)
    near_y = tuple(jnp.logical_and(a, jnp.logical_not(b)) for a, b in zip(has_y, far_y))
    step = (-1, 1)
    zs, rest = 4, nn // 4
    groups = modes // GROUP

    def u_load(g):
        s = pl.ds(g * GROUP, GROUP)
        return pltpu.make_async_copy(u_hbm.at[s], u.at[s, :, pl.ds(1, nx)], load_sem.at[g])

    def v_load(g):
        s = pl.ds(g * GROUP, GROUP)
        return pltpu.make_async_copy(v_hbm.at[s], v.at[s], load_sem.at[groups + g])

    base_load = pltpu.make_async_copy(base_hbm, base.at[:, pl.ds(1, nx)], load_sem.at[2 * groups])
    cell_load = pltpu.make_async_copy(cell_hbm, cell, load_sem.at[2 * groups + 1])
    mix_load = pltpu.make_async_copy(mix_hbm, mix, load_sem.at[2 * groups + 2])
    mix_load.start()
    for g in range(groups):
        u_load(g).start()
    base_load.start()
    cell_load.start()
    for g in range(groups):
        v_load(g).start()

    first = [(lax.rem(c + k, nc), n) for k in range(1, nc)]
    second = [(c, n // zs * zs + lax.rem(lax.rem(n, zs) + k, zs)) for k in range(1, zs)]
    third = [(c, lax.rem(n // zs + k, rest) * zs + lax.rem(n, zs)) for k in range(1, rest)]
    around = [(c, lax.rem(n + 1, nn)), (c, lax.rem(n + nn - 1, nn))]
    barrier = pltpu.get_barrier_semaphore()
    peers = first + second + third + around
    for peer in peers:
        pl.semaphore_signal(barrier, inc=1, device_id=peer, device_id_type=MESH)

    @pl.when(c == 0)
    def _():
        u[:, :, 0] = jnp.zeros((modes, nv, ny, nz), BF16)
        base[:, 0] = jnp.zeros((nv, ny, nz), F32)
        sx[:, 0] = jnp.zeros((nv, ny, nz), F32)
        field[0, :, 0] = jnp.zeros((nv, ny, nz), F32)
        field[1, :, 0] = jnp.zeros((nv, ny, nz), F32)

    @pl.when(c == nc - 1)
    def _():
        u[:, :, nx + 1] = jnp.zeros((modes, nv, ny, nz), BF16)
        base[:, nx + 1] = jnp.zeros((nv, ny, nz), F32)
        sx[:, 3] = jnp.zeros((nv, ny, nz), F32)
        field[0, :, nx + 1] = jnp.zeros((nv, ny, nz), F32)
        field[1, :, nx + 1] = jnp.zeros((nv, ny, nz), F32)

    for side, at_edge in ((0, n == 0), (1, n == nn - 1)):
        @pl.when(at_edge)
        def _():
            uhalo[side] = jnp.zeros((modes, nv, nx, nz), BF16)
            bhalo[side] = jnp.zeros((nv, nx, nz), F32)
            shalo[side] = jnp.zeros((nv, nx, nz), F32)
            yhalo[0, side] = jnp.zeros((nv, nx, nz), F32)
            yhalo[1, side] = jnp.zeros((nv, nx, nz), F32)

    pl.semaphore_wait(barrier, len(peers))

    def x_copy(kind, way, src, dst):
        return pltpu.make_async_remote_copy(
            src_ref=src, dst_ref=dst, send_sem=xs_sem.at[kind, way], recv_sem=xr_sem.at[kind, 1 - way],
            device_id=(lax.rem(c + step[way] + nc, nc), n), device_id_type=MESH)

    def y_copy(kind, way, src, dst):
        return pltpu.make_async_remote_copy(
            src_ref=src, dst_ref=dst, send_sem=ys_sem.at[kind, way], recv_sem=yr_sem.at[kind, 1 - way],
            device_id=(c, lax.rem(n + step[way] + nn, nn)), device_id_type=MESH)

    front, back = pl.ds(0, modes // 2), pl.ds(modes // 2, modes // 2)
    x_links = [
        lambda w: x_copy(0, w, u_hbm.at[front, :, (nx - 1) * w], u.at[front, :, (nx + 1) * (1 - w)]),
        lambda w: x_copy(1, w, base_hbm.at[:, (nx - 1) * w], base.at[:, (nx + 1) * (1 - w)]),
        lambda w: x_copy(2, w, sx.at[:, 1 + w], sx.at[:, 3 * (1 - w)]),
        lambda w: x_copy(3, w, field.at[0, :, 1 + (nx - 1) * w], field.at[0, :, (nx + 1) * (1 - w)]),
        lambda w: x_copy(4, w, field.at[1, :, 1 + (nx - 1) * w], field.at[1, :, (nx + 1) * (1 - w)]),
        lambda w: x_copy(5, w, u_hbm.at[back, :, (nx - 1) * w], u.at[back, :, (nx + 1) * (1 - w)]),
    ]
    y_links = [
        lambda w: y_copy(0, w, bface.at[w], bhalo.at[1 - w]),
        lambda w: y_copy(1, w, sface.at[w], shalo.at[1 - w]),
        lambda w: y_copy(2, w, ysend.at[0, w], yhalo.at[0, 1 - w]),
        lambda w: y_copy(3, w, ysend.at[1, w], yhalo.at[1, 1 - w]),
        lambda w: y_copy(4, w, uface.at[w, pl.ds(0, GROUP)], uhalo.at[1 - w, pl.ds(0, GROUP)]),
        lambda w: y_copy(5, w, uface.at[w, pl.ds(GROUP, modes - GROUP)], uhalo.at[1 - w, pl.ds(GROUP, modes - GROUP)]),
    ]

    def send(link, has):
        for w in (0, 1):
            @pl.when(has[w])
            def _():
                link(w).start()

    def receive(link, has):
        for side in (0, 1):
            @pl.when(has[side])
            def _():
                link(1 - side).wait_recv()

    def drain(link, has):
        for w in (0, 1):
            @pl.when(has[w])
            def _():
                link(w).wait_send()

    pick_row = iota((2 * nx, nx * ny), 0)
    from_row = iota((2 * nx, nx * ny), 1)
    wanted = jnp.where(pick_row < nx, pick_row * ny, (pick_row - nx) * ny + ny - 1)
    select[...] = jnp.where(from_row == wanted, 1.0, 0.0).astype(BF16)
    lane_in, lane_out = iota((nz, nz), 0), iota((nz, nz), 1)
    ahead = jnp.where(lane_out == nz - 1, 0, lane_out + 1)
    behind = jnp.where(lane_out == 0, nz - 1, lane_out - 1)
    circ[...] = (jnp.where(lane_in == ahead, 1.0, 0.0) - jnp.where(lane_in == behind, 1.0, 0.0)).astype(BF16)

    def faces_of(block, faces, m):
        for i in range(nv):
            both = dot(select[...], block(m, i).reshape(nx * ny, nz))
            faces[0, m, i] = both[:nx].astype(BF16)
            faces[1, m, i] = both[nx:].astype(BF16)

    for g in range(groups):
        u_load(g).wait()

        def u_mode(m, carry):
            total = jnp.zeros((ny, nz), F32)
            for i in range(nv):
                for x in range(nx):
                    cells = u[m, i, 1 + x].astype(F32)
                    total = total + cells * cells
            total = jnp.sum(total, axis=0, keepdims=True)
            energy[pl.ds(m, 1), :] = total[:, :128] + total[:, 128:]
            faces_of(lambda m, i: u[m, i, pl.ds(1, nx)], uface, m)
            return carry

        lax.fori_loop(g * GROUP, (g + 1) * GROUP, u_mode, 0)
        if g == 0:
            send(y_links[4], far_y)

    def e_copy(index, peer, dst):
        return pltpu.make_async_remote_copy(
            src_ref=energy.at[pl.ds(modes * (0 if index < nc - 1 else 1 if index < nc + zs - 2 else 2), modes)],
            dst_ref=dst, send_sem=es_sem.at[index], recv_sem=er_sem.at[index], device_id=peer, device_id_type=MESH)

    ones = [e_copy(k, first[k], round_one.at[k]) for k in range(nc - 1)]
    twos = [e_copy(nc - 1 + k, second[k], round_two.at[k]) for k in range(zs - 1)]
    threes = [e_copy(nc + zs - 2 + k, third[k], round_three.at[k]) for k in range(rest - 1)]

    def v_faces(g):
        v_load(g).wait()

        def v_mode(m, carry):
            faces_of(lambda m, i: v[m, i], vface, m)
            return carry

        lax.fori_loop(g * GROUP, (g + 1) * GROUP, v_mode, 0, unroll=2)

    def finish(copies, slots, src):
        total = energy[pl.ds(modes * src, modes), :]
        for k, copy in enumerate(copies):
            copy.wait_recv()
            total = total + slots[k]
        return total

    for copy in ones:
        copy.start()
    v_faces(0)
    energy[pl.ds(modes, modes), :] = finish(ones, round_one, 0)
    for copy in twos:
        copy.start()

    mix_load.wait()
    width = 3 * kv
    lane = iota((ny, width), 1)
    row = iota((ny, width), 0)
    lane_row = lax.rem(lane, ny)
    lane_var = lax.rem(lane, kv) // ny
    same = jnp.where(lane_row == row, 1.0, 0.0)
    nxt = jnp.where(lane_row == row + 1, 1.0, 0.0)
    prv = jnp.where(lane_row == row - 1, 1.0, 0.0)
    kinds = ((0, same), (1, nxt - same), (1, same - prv), (2, same), (1, same))
    table = [mix[i] for i in range(nv)]
    for k, (d, stencil) in enumerate(kinds):
        for j in range(nv):
            coefs = jnp.zeros((ny, width), F32)
            for i in range(nv):
                coefs = jnp.where(lane_var == i, table[i][d : d + 1, j : j + 1], coefs)
            mat0[pl.ds((k * nv + j) * ny, ny), :] = coefs * stencil
    high = mat0[...].astype(BF16)
    low = (mat0[...] - high.astype(F32)).astype(BF16)
    mat2[...] = jnp.where(iota(mat0.shape, 1) < 2 * kv, high.astype(F32), low.astype(F32)).astype(BF16)

    v_faces(1)
    energy[pl.ds(2 * modes, modes), :] = finish(twos, round_two, 1)
    for copy in threes:
        copy.start()
    v_faces(2)

    cell_load.wait()
    base_load.wait()
    kind_of = cell[...]
    weight[...] = jnp.where(kind_of == 0, 1.0, jnp.where(kind_of == 1, 0.5, 0.0)).astype(F32)
    for side in (0, 1):
        for x in range(nx):
            bface[side, :, pl.ds(x, 1), :] = base[:, 1 + x, pl.ds((ny - 1) * side, 1), :]

    def base_plane(x, carry):
        for j in range(nv):
            base_dz[j, x] = diff_lanes(base[j, 1 + x])
        return carry

    lax.fori_loop(0, nx, base_plane, 0)
    v_faces(3)

    cells_all = nc * nn * nv * nx * ny * nz
    total = jnp.sum(finish(threes, round_three, 2), axis=1, keepdims=True)
    send(y_links[5], far_y)
    send(x_links[0], has_x)
    send(x_links[5], has_x)
    send(y_links[4], near_y)
    send(y_links[5], near_y)
    send(x_links[1], has_x)
    send(y_links[0], has_y)
    amp[...] = jnp.broadcast_to(lax.rsqrt(total / cells_all + 1e-06) / modes, amp.shape)

    def mode_matrix(m, carry):
        scaled = mat0[:, pl.ds(0, 2 * kv)] * amp[pl.ds(m, 1), pl.ds(0, 2 * kv)]
        big = scaled.astype(BF16).astype(F32)
        mats[m] = jnp.where(iota(scaled.shape, 1) < kv, big, scaled - big).astype(BF16)
        return carry

    lax.fori_loop(0, modes, mode_matrix, 0)

    sface[...] = jnp.zeros(sface.shape, F32)
    sx[:, 1] = jnp.zeros((nv, ny, nz), F32)
    sx[:, 2] = jnp.zeros((nv, ny, nz), F32)

    def face_group(g, carry):
        m0 = g * GROUP
        for s in (0, 1):
            x = 1 + (nx - 1) * s
            for k in range(GROUP):
                rows = vface[s, pick[m0 + k]].reshape(kv, nz)
                wface[s, m0 + k] = dot(mats[m0 + k, pl.ds(4 * kv, kv), :], jnp.concatenate([rows, rows], axis=0))
                rows = v[pick[m0 + k], :, x - 1].reshape(kv, nz)
                w_scr[s, k, pl.ds(0, kv), :] = dot(mats[m0 + k, pl.ds(0, kv), :], jnp.concatenate([rows, rows], axis=0))
        for s in (0, 1):
            x = 1 + (nx - 1) * s
            for j in range(nv):
                r = pl.ds(j * ny, ny)
                at_face, at_end = sface[s, j], sx[j, 1 + s]
                for k in range(GROUP):
                    at_face = at_face + wface[s, m0 + k, pl.ds(j * nx, nx), :] * uface[s, m0 + k, j].astype(F32)
                    at_end = at_end + w_scr[s, k, r, :] * u[m0 + k, j, x].astype(F32)
                sface[s, j] = at_face
                sx[j, 1 + s] = at_end
        return carry

    lax.fori_loop(0, groups, face_group, 0)
    send(x_links[2], has_x)
    send(y_links[1], has_y)

    def mix_part(x, g, slot, k):
        m0 = g * MG
        if k == MG:
            du_scr[slot] = dot(u[pl.ds(m0, MG), :, x].reshape(MG * kv, nz), circ[...])
        elif k < MG:
            rows = v[pick[m0 + k], :, x - 1].reshape(kv, nz)
            w_scr[slot, k] = dot(mats[m0 + k, pl.ds(0, 4 * kv), :], jnp.concatenate([rows, rows], axis=0))

    def mix_group(x, g, slot):
        for k in range(MG + 1):
            mix_part(x, g, slot, k)

    def plane_of(t):
        return lax.rem(t + 1, nx) + 1

    def plane(t, carry):
        x = plane_of(t)
        for g in range((modes // MG)):
            slot = g % 2
            for j in range(nv):
                for part in range(j, MG + 1, nv):
                    if g < (modes // MG) - 1:
                        mix_part(x, g + 1, 1 - slot, part)
                    else:
                        mix_part(plane_of(t + 1), 0, 1 - slot, part)
                for h in (0, 1):
                    z = pl.ds(128 * h, 128)
                    if g == 0:
                        q = s_x = s_z = up = down = jnp.zeros((ny, 128), F32)
                    else:
                        q, s_x, s_z, up, down = (acc[i, j, :, z] for i in range(5))
                    for k in range(MG):
                        m = g * MG + k
                        here = u[m, j, x, :, z].astype(F32)
                        dx = u[m, j, x + 1, :, z].astype(F32) - u[m, j, x - 1, :, z].astype(F32)
                        dz = du_scr[slot, pl.ds(k * kv + j * ny, ny), z]
                        wx, wp, wm, wz = (w_scr[slot, k, pl.ds(i * kv + j * ny, ny), z] for i in range(4))
                        q = q + dx * wx + dz * wz
                        s_x = s_x + here * wx
                        s_z = s_z + here * wz
                        up = up + here * wm
                        down = down + here * wp
                    for i, value in enumerate((q, s_x, s_z, up, down)):
                        acc[i, j, :, z] = value
                if g == (modes // MG) - 1:
                    grad[j, x - 1] = acc[0, j] - diff_lanes(acc[2, j]) - rows_up(acc[3, j]) - rows_down(acc[4, j])
                    sx_all[j, x - 1] = acc[1, j]
        return carry

    mix_group(plane_of(0), 0, 0)
    lax.fori_loop(0, nx - 2, plane, 0)
    receive(x_links[0], has_x)
    receive(x_links[5], has_x)
    lax.fori_loop(nx - 2, nx, plane, 0)

    receive(x_links[2], has_x)
    for j in range(nv):
        field[0, j, 1] = weight[0] * (grad[j, 0] - (sx_all[j, 1] - sx[j, 0]))
        field[0, j, nx] = weight[nx - 1] * (grad[j, nx - 1] - (sx[j, 3] - sx_all[j, nx - 2]))

    def grad_plane(x, carry):
        for j in range(nv):
            field[0, j, x + 1] = weight[x] * (grad[j, x] - (sx_all[j, x + 1] - sx_all[j, x - 1]))
        return carry

    lax.fori_loop(1, nx - 1, grad_plane, 0, unroll=2)
    receive(y_links[4], has_y)
    receive(y_links[1], has_y)

    def cross(first_mode, last_mode):
        def terms(j, carry):
            for s in (0, 1):
                value = (shalo if first_mode == 0 else fterm)[s, j]
                value = -value if first_mode == 0 and s == 1 else value
                for m in range(first_mode, last_mode):
                    term = wface[s, m, pl.ds(pl.multiple_of(j * nx, nx), nx), :] * uhalo[s, m, j].astype(F32)
                    value = value - term if s == 0 else value + term
                fterm[s, j] = value
            return carry

        lax.fori_loop(0, nv, terms, 0)

    cross(0, GROUP)
    receive(y_links[5], has_y)
    cross(GROUP, modes)

    def add_rows(target, x0, weighted):
        for side in (0, 1):
            end = pl.ds((ny - 1) * side, 1)
            for x in range(nx):
                change = fterm[side, :, pl.ds(x, 1), :]
                if weighted:
                    change = change * weight[x, end, :]
                target[:, x + x0, end, :] = target[:, x + x0, end, :] + change

    add_rows(field.at[0], 1, True)

    def apply(slot):
        target = field.at[1] if slot == 0 else grad
        shift = 0 if slot == 0 else 1
        for side in (0, 1):
            for x in range(nx):
                ysend[slot, side, :, pl.ds(x, 1), :] = field[slot, :, 1 + x, pl.ds((ny - 1) * side, 1), :]
        send(y_links[2 + slot], has_y)
        send(x_links[3 + slot], has_x)

        def mixed(x, carry):
            wall[x] = dot(mat2[pl.ds(0, 4 * kv), :], split3(field[slot, :, x].reshape(kv, nz)))
            return carry

        lax.fori_loop(1, nx + 1, mixed, 0, unroll=4)
        for s in (0, 1):
            wface[s, 0] = dot(mat2[pl.ds(4 * kv, kv), :], split3(ysend[slot, s].reshape(kv, nz)))

        def result_plane(x, carry):
            for j in range(nv):
                r = pl.ds(j * ny, ny)
                wx = wall[x, r, :]
                wp, wm, wz = (wall[x, pl.ds(t * kv + j * ny, ny), :] for t in (1, 2, 3))
                here = base[j, x]
                value = base[j, x + 1] * (wx - wall[x + 1, r, :]) - base[j, x - 1] * (wx - wall[x - 1, r, :])
                value = value + base_dz[j, x - 1] * wz - diff_lanes(here * wz)
                value = value - rows_up(here * wm) - rows_down(here * wp)
                target[j, x - shift] = weight[x - 1] * value if slot == 0 else -value
            return carry

        lax.fori_loop(2, nx, result_plane, 0, unroll=2)
        if slot == 0:
            receive(x_links[1], has_x)
            receive(y_links[0], has_y)
        receive(y_links[2 + slot], has_y)
        for s in (0, 1):
            far_side = dot(mat2[pl.ds(4 * kv, kv), :], split3(yhalo[slot, s].reshape(kv, nz)))
            change = (far_side - wface[s, 0]).reshape(nv, nx, nz) * bhalo[s]
            fterm[s] = change if s == slot else -change
        receive(x_links[3 + slot], has_x)
        for x in (0, nx + 1):
            wall[x, pl.ds(0, kv), :] = dot(mat2[pl.ds(0, kv), :], split3(field[slot, :, x].reshape(kv, nz)))
        lax.fori_loop(0, 2, lambda s, carry: result_plane(1 + (nx - 1) * s, carry), 0, unroll=2)
        add_rows(target, 1 - shift, slot == 0)

    apply(0)
    apply(1)
    store = pltpu.make_async_copy(grad, out_hbm, out_sem)
    store.start()
    for link in x_links:
        drain(link, has_x)
    for link in y_links:
        drain(link, has_y)
    for copy in ones + twos + threes:
        copy.wait_send()
    store.wait()


def per_device(u, v, base, cell, pick, mix, *, interpret=False):
    modes, nv, nx, ny, nz = u.shape
    nc, nn = lax.axis_size("chord"), lax.axis_size("normal")
    kv = nv * ny
    groups = modes // GROUP
    vm = pltpu.VMEM
    any_space = pl.BlockSpec(memory_space=pl.ANY)
    smem = pl.BlockSpec(memory_space=pltpu.SMEM)
    negated = pl.pallas_call(
        functools.partial(kernel, (nc, nn, modes, nv, nx, ny, nz)),
        out_shape=jax.ShapeDtypeStruct(base.shape, F32),
        in_specs=[any_space] * 5 + [smem],
        out_specs=any_space,
        scratch_shapes=[
            vm((modes, nv, nx + 2, ny, nz), BF16),
            vm((modes, nv, nx, ny, nz), BF16),
            vm((nv, nx + 2, ny, nz), F32),
            vm((nx, ny, nz), jnp.int32),
            vm((nv, 3, nv), F32),
            vm((2, modes, nv, nx, nz), BF16),
            vm((2, modes, nv, nx, nz), BF16),
            vm((2, modes, nv, nx, nz), BF16),
            vm((2, modes, kv, nz), F32),
            vm((modes, 5 * kv, 2 * kv), BF16),
            vm((5 * kv, 3 * kv), BF16),
            vm((5 * kv, 3 * kv), F32),
            vm((2 * nx, nx * ny), BF16),
            vm((nz, nz), BF16),
            vm((2, max(GROUP, MG), 4 * kv, nz), F32),
            vm((2, MG * kv, nz), F32),
            vm((5, nv, ny, nz), F32),
            vm((nv, nx, ny, nz), F32),
            vm((nv, 4, ny, nz), F32),
            vm((nv, nx, ny, nz), F32),
            vm((2, nv, nx, nz), F32),
            vm((2, nv, nx, nz), F32),
            vm((2, 2, nv, nx, nz), F32),
            vm((2, 2, nv, nx, nz), F32),
            vm((2, nv, nx + 2, ny, nz), F32),
            vm((nx + 2, 4 * kv, nz), F32),
            vm((nv, nx, ny, nz), F32),
            vm((2, nv, nx, nz), F32),
            vm((2, nv, nx, nz), F32),
            vm((2, nv, nx, nz), F32),
            vm((3 * modes, 128), F32),
            vm((nc - 1, modes, 128), F32),
            vm((3, modes, 128), F32),
            vm((max(nn // 4 - 1, 1), modes, 128), F32),
            vm((modes, 256), F32),
            vm((nx, ny, nz), F32),
            pltpu.SemaphoreType.DMA((2 * groups + 3,)),
            pltpu.SemaphoreType.DMA((6, 2)),
            pltpu.SemaphoreType.DMA((6, 2)),
            pltpu.SemaphoreType.DMA((6, 2)),
            pltpu.SemaphoreType.DMA((6, 2)),
            pltpu.SemaphoreType.DMA((nc + nn // 4 + 1,)),
            pltpu.SemaphoreType.DMA((nc + nn // 4 + 1,)),
            pltpu.SemaphoreType.DMA,
        ],
        compiler_params=pltpu.CompilerParams(
            collective_id=0, has_side_effects=True, vmem_limit_bytes=60 * 2**20),
    )(u, v, base, cell, mix.transpose(1, 0, 2), pick)
    return -negated


def solution(mesh):
    return jax.shard_map(
        per_device,
        mesh=mesh,
        in_specs=(
            P(None, None, "chord", "normal", None),
            P(None, None, "chord", "normal", None),
            P(None, "chord", "normal", None),
            P("chord", "normal", None),
            P(),
            P(),
        ),
        out_specs=P(None, "chord", "normal", None),
        check_vma=False,
    )
```

```python
import functools

import jax
import jax.numpy as jnp
from jax import lax
from jax.experimental import pallas as pl
from jax.experimental.pallas import tpu as pltpu
from jax.sharding import PartitionSpec as P

MESH = pl.DeviceIdType.MESH
F32 = jnp.float32
BF16 = jnp.bfloat16
GROUP = 4
MG = 2


def iota(shape, dim):
    return lax.broadcasted_iota(jnp.int32, shape, dim)


def diff_lanes(x):
    lanes = x.shape[-1]
    return pltpu.roll(x, lanes - 1, 1) - pltpu.roll(x, 1, 1)


def rows_up(x):
    rows = x.shape[0]
    return jnp.where(iota(x.shape, 0) == rows - 1, 0.0, pltpu.roll(x, rows - 1, 0))


def rows_down(x):
    return jnp.where(iota(x.shape, 0) == 0, 0.0, pltpu.roll(x, 1, 0))


def split3(x):
    high = x.astype(BF16)
    low = (x - high.astype(F32)).astype(BF16)
    return jnp.concatenate([high, low, high], axis=0)


def dot(a, b):
    return jnp.dot(a, b, preferred_element_type=F32)


def kernel(
    sizes,
    u_hbm, v_hbm, base_hbm, cell_hbm, mix_hbm, pick,
    out_hbm,
    u, v, base, cell, mix, uface, vface, uhalo, wface, mats, mat2, mat0, select, circ,
    w_scr, du_scr, acc, grad, sx, sx_all, sface, shalo, ysend, yhalo, field, wall, base_dz, bface, bhalo,
    fterm, energy, round_one, round_two, round_three, amp, weight,
    load_sem, xs_sem, xr_sem, ys_sem, yr_sem, es_sem, er_sem, out_sem,
):
    nc, nn, modes, nv, nx, ny, nz = sizes
    kv = nv * ny
    c, n = lax.axis_index("chord"), lax.axis_index("normal")
    has_x = (c > 0, c < nc - 1)
    has_y = (n > 0, n < nn - 1)
    half = nn // 2
    far_y = (n == half, n == half - 1)
    near_y = tuple(jnp.logical_and(a, jnp.logical_not(b)) for a, b in zip(has_y, far_y))
    step = (-1, 1)
    zs, rest = 4, nn // 4
    groups = modes // GROUP

    def u_load(g):
        s = pl.ds(g * GROUP, GROUP)
        return pltpu.make_async_copy(u_hbm.at[s], u.at[s, :, pl.ds(1, nx)], load_sem.at[g])

    def v_load(g):
        s = pl.ds(g * GROUP, GROUP)
        return pltpu.make_async_copy(v_hbm.at[s], v.at[s], load_sem.at[groups + g])

    base_load = pltpu.make_async_copy(base_hbm, base.at[:, pl.ds(1, nx)], load_sem.at[2 * groups])
    cell_load = pltpu.make_async_copy(cell_hbm, cell, load_sem.at[2 * groups + 1])
    mix_load = pltpu.make_async_copy(mix_hbm, mix, load_sem.at[2 * groups + 2])
    mix_load.start()
    for g in range(groups):
        u_load(g).start()
    base_load.start()
    cell_load.start()
    for g in range(groups):
        v_load(g).start()

    first = [(lax.rem(c + k, nc), n) for k in range(1, nc)]
    second = [(c, n // zs * zs + lax.rem(lax.rem(n, zs) + k, zs)) for k in range(1, zs)]
    third = [(c, lax.rem(n // zs + k, rest) * zs + lax.rem(n, zs)) for k in range(1, rest)]
    around = [(c, lax.rem(n + 1, nn)), (c, lax.rem(n + nn - 1, nn))]
    barrier = pltpu.get_barrier_semaphore()
    peers = first + second + third + around
    for peer in peers:
        pl.semaphore_signal(barrier, inc=1, device_id=peer, device_id_type=MESH)

    @pl.when(c == 0)
    def _():
        u[:, :, 0] = jnp.zeros((modes, nv, ny, nz), BF16)
        base[:, 0] = jnp.zeros((nv, ny, nz), F32)
        sx[:, 0] = jnp.zeros((nv, ny, nz), F32)
        field[0, :, 0] = jnp.zeros((nv, ny, nz), F32)
        field[1, :, 0] = jnp.zeros((nv, ny, nz), F32)

    @pl.when(c == nc - 1)
    def _():
        u[:, :, nx + 1] = jnp.zeros((modes, nv, ny, nz), BF16)
        base[:, nx + 1] = jnp.zeros((nv, ny, nz), F32)
        sx[:, 3] = jnp.zeros((nv, ny, nz), F32)
        field[0, :, nx + 1] = jnp.zeros((nv, ny, nz), F32)
        field[1, :, nx + 1] = jnp.zeros((nv, ny, nz), F32)

    for side, at_edge in ((0, n == 0), (1, n == nn - 1)):
        @pl.when(at_edge)
        def _():
            uhalo[side] = jnp.zeros((modes, nv, nx, nz), BF16)
            bhalo[side] = jnp.zeros((nv, nx, nz), F32)
            shalo[side] = jnp.zeros((nv, nx, nz), F32)
            yhalo[0, side] = jnp.zeros((nv, nx, nz), F32)
            yhalo[1, side] = jnp.zeros((nv, nx, nz), F32)

    pl.semaphore_wait(barrier, len(peers))

    def x_copy(kind, way, src, dst):
        return pltpu.make_async_remote_copy(
            src_ref=src, dst_ref=dst, send_sem=xs_sem.at[kind, way], recv_sem=xr_sem.at[kind, 1 - way],
            device_id=(lax.rem(c + step[way] + nc, nc), n), device_id_type=MESH)

    def y_copy(kind, way, src, dst):
        return pltpu.make_async_remote_copy(
            src_ref=src, dst_ref=dst, send_sem=ys_sem.at[kind, way], recv_sem=yr_sem.at[kind, 1 - way],
            device_id=(c, lax.rem(n + step[way] + nn, nn)), device_id_type=MESH)

    front, back = pl.ds(0, modes // 2), pl.ds(modes // 2, modes // 2)
    x_links = [
        lambda w: x_copy(0, w, u_hbm.at[front, :, (nx - 1) * w], u.at[front, :, (nx + 1) * (1 - w)]),
        lambda w: x_copy(1, w, base_hbm.at[:, (nx - 1) * w], base.at[:, (nx + 1) * (1 - w)]),
        lambda w: x_copy(2, w, sx.at[:, 1 + w], sx.at[:, 3 * (1 - w)]),
        lambda w: x_copy(3, w, field.at[0, :, 1 + (nx - 1) * w], field.at[0, :, (nx + 1) * (1 - w)]),
        lambda w: x_copy(4, w, field.at[1, :, 1 + (nx - 1) * w], field.at[1, :, (nx + 1) * (1 - w)]),
        lambda w: x_copy(5, w, u_hbm.at[back, :, (nx - 1) * w], u.at[back, :, (nx + 1) * (1 - w)]),
    ]
    y_links = [
        lambda w: y_copy(0, w, bface.at[w], bhalo.at[1 - w]),
        lambda w: y_copy(1, w, sface.at[w], shalo.at[1 - w]),
        lambda w: y_copy(2, w, ysend.at[0, w], yhalo.at[0, 1 - w]),
        lambda w: y_copy(3, w, ysend.at[1, w], yhalo.at[1, 1 - w]),
        lambda w: y_copy(4, w, uface.at[w, front], uhalo.at[1 - w, front]),
        lambda w: y_copy(5, w, uface.at[w, back], uhalo.at[1 - w, back]),
    ]

    def send(link, has):
        for w in (0, 1):
            @pl.when(has[w])
            def _():
                link(w).start()

    def receive(link, has):
        for side in (0, 1):
            @pl.when(has[side])
            def _():
                link(1 - side).wait_recv()

    def drain(link, has):
        for w in (0, 1):
            @pl.when(has[w])
            def _():
                link(w).wait_send()

    pick_row = iota((2 * nx, nx * ny), 0)
    from_row = iota((2 * nx, nx * ny), 1)
    wanted = jnp.where(pick_row < nx, pick_row * ny, (pick_row - nx) * ny + ny - 1)
    select[...] = jnp.where(from_row == wanted, 1.0, 0.0).astype(BF16)
    lane_in, lane_out = iota((nz, nz), 0), iota((nz, nz), 1)
    ahead = jnp.where(lane_out == nz - 1, 0, lane_out + 1)
    behind = jnp.where(lane_out == 0, nz - 1, lane_out - 1)
    circ[...] = (jnp.where(lane_in == ahead, 1.0, 0.0) - jnp.where(lane_in == behind, 1.0, 0.0)).astype(BF16)

    def faces_of(block, faces, m):
        for i in range(nv):
            both = dot(select[...], block(m, i).reshape(nx * ny, nz))
            faces[0, m, i] = both[:nx].astype(BF16)
            faces[1, m, i] = both[nx:].astype(BF16)

    for g in range(groups):
        u_load(g).wait()

        def u_mode(m, carry):
            total = jnp.zeros((ny, nz), F32)
            for i in range(nv):
                for x in range(nx):
                    cells = u[m, i, 1 + x].astype(F32)
                    total = total + cells * cells
            total = jnp.sum(total, axis=0, keepdims=True)
            energy[pl.ds(m, 1), :] = total[:, :128] + total[:, 128:]
            faces_of(lambda m, i: u[m, i, pl.ds(1, nx)], uface, m)
            return carry

        lax.fori_loop(g * GROUP, (g + 1) * GROUP, u_mode, 0)
        if g == groups // 2 - 1:
            send(y_links[4], far_y)

    def e_copy(index, peer, dst):
        return pltpu.make_async_remote_copy(
            src_ref=energy.at[pl.ds(modes * (0 if index < nc - 1 else 1 if index < nc + zs - 2 else 2), modes)],
            dst_ref=dst, send_sem=es_sem.at[index], recv_sem=er_sem.at[index], device_id=peer, device_id_type=MESH)

    ones = [e_copy(k, first[k], round_one.at[k]) for k in range(nc - 1)]
    twos = [e_copy(nc - 1 + k, second[k], round_two.at[k]) for k in range(zs - 1)]
    threes = [e_copy(nc + zs - 2 + k, third[k], round_three.at[k]) for k in range(rest - 1)]

    def v_faces(g):
        v_load(g).wait()

        def v_mode(m, carry):
            faces_of(lambda m, i: v[m, i], vface, m)
            return carry

        lax.fori_loop(g * GROUP, (g + 1) * GROUP, v_mode, 0, unroll=2)

    def finish(copies, slots, src):
        total = energy[pl.ds(modes * src, modes), :]
        for k, copy in enumerate(copies):
            copy.wait_recv()
            total = total + slots[k]
        return total

    for copy in ones:
        copy.start()
    v_faces(0)
    energy[pl.ds(modes, modes), :] = finish(ones, round_one, 0)
    for copy in twos:
        copy.start()

    mix_load.wait()
    width = 3 * kv
    lane = iota((ny, width), 1)
    row = iota((ny, width), 0)
    lane_row = lax.rem(lane, ny)
    lane_var = lax.rem(lane, kv) // ny
    same = jnp.where(lane_row == row, 1.0, 0.0)
    nxt = jnp.where(lane_row == row + 1, 1.0, 0.0)
    prv = jnp.where(lane_row == row - 1, 1.0, 0.0)
    kinds = ((0, same), (1, nxt - same), (1, same - prv), (2, same), (1, same))
    table = [mix[i] for i in range(nv)]
    for k, (d, stencil) in enumerate(kinds):
        for j in range(nv):
            coefs = jnp.zeros((ny, width), F32)
            for i in range(nv):
                coefs = jnp.where(lane_var == i, table[i][d : d + 1, j : j + 1], coefs)
            mat0[pl.ds((k * nv + j) * ny, ny), :] = coefs * stencil
    high = mat0[...].astype(BF16)
    low = (mat0[...] - high.astype(F32)).astype(BF16)
    mat2[...] = jnp.where(iota(mat0.shape, 1) < 2 * kv, high.astype(F32), low.astype(F32)).astype(BF16)

    v_faces(1)
    energy[pl.ds(2 * modes, modes), :] = finish(twos, round_two, 1)
    for copy in threes:
        copy.start()
    v_faces(2)

    cell_load.wait()
    base_load.wait()
    kind_of = cell[...]
    weight[...] = jnp.where(kind_of == 0, 1.0, jnp.where(kind_of == 1, 0.5, 0.0)).astype(F32)
    for side in (0, 1):
        for x in range(nx):
            bface[side, :, pl.ds(x, 1), :] = base[:, 1 + x, pl.ds((ny - 1) * side, 1), :]

    def base_plane(x, carry):
        for j in range(nv):
            base_dz[j, x] = diff_lanes(base[j, 1 + x])
        return carry

    lax.fori_loop(0, nx, base_plane, 0)
    v_faces(3)

    cells_all = nc * nn * nv * nx * ny * nz
    total = jnp.sum(finish(threes, round_three, 2), axis=1, keepdims=True)
    send(y_links[5], far_y)
    send(x_links[0], has_x)
    send(x_links[5], has_x)
    send(y_links[4], near_y)
    send(y_links[5], near_y)
    send(x_links[1], has_x)
    send(y_links[0], has_y)
    amp[...] = jnp.broadcast_to(lax.rsqrt(total / cells_all + 1e-06) / modes, amp.shape)

    def mode_matrix(m, carry):
        scaled = mat0[:, pl.ds(0, 2 * kv)] * amp[pl.ds(m, 1), pl.ds(0, 2 * kv)]
        big = scaled.astype(BF16).astype(F32)
        mats[m] = jnp.where(iota(scaled.shape, 1) < kv, big, scaled - big).astype(BF16)
        return carry

    lax.fori_loop(0, modes, mode_matrix, 0)

    sface[...] = jnp.zeros(sface.shape, F32)
    sx[:, 1] = jnp.zeros((nv, ny, nz), F32)
    sx[:, 2] = jnp.zeros((nv, ny, nz), F32)

    def face_group(g, carry):
        m0 = g * GROUP
        for s in (0, 1):
            x = 1 + (nx - 1) * s
            for k in range(GROUP):
                rows = vface[s, pick[m0 + k]].reshape(kv, nz)
                wface[s, m0 + k] = dot(mats[m0 + k, pl.ds(4 * kv, kv), :], jnp.concatenate([rows, rows], axis=0))
                rows = v[pick[m0 + k], :, x - 1].reshape(kv, nz)
                w_scr[s, k, pl.ds(0, kv), :] = dot(mats[m0 + k, pl.ds(0, kv), :], jnp.concatenate([rows, rows], axis=0))
        for s in (0, 1):
            x = 1 + (nx - 1) * s
            for j in range(nv):
                r = pl.ds(j * ny, ny)
                at_face, at_end = sface[s, j], sx[j, 1 + s]
                for k in range(GROUP):
                    at_face = at_face + wface[s, m0 + k, pl.ds(j * nx, nx), :] * uface[s, m0 + k, j].astype(F32)
                    at_end = at_end + w_scr[s, k, r, :] * u[m0 + k, j, x].astype(F32)
                sface[s, j] = at_face
                sx[j, 1 + s] = at_end
        return carry

    lax.fori_loop(0, groups, face_group, 0)
    send(x_links[2], has_x)
    send(y_links[1], has_y)

    def mix_part(x, g, slot, k):
        m0 = g * MG
        if k == MG:
            du_scr[slot] = dot(u[pl.ds(m0, MG), :, x].reshape(MG * kv, nz), circ[...])
        elif k < MG:
            rows = v[pick[m0 + k], :, x - 1].reshape(kv, nz)
            w_scr[slot, k] = dot(mats[m0 + k, pl.ds(0, 4 * kv), :], jnp.concatenate([rows, rows], axis=0))

    def mix_group(x, g, slot):
        for k in range(MG + 1):
            mix_part(x, g, slot, k)

    def plane_of(t):
        return lax.rem(t + 1, nx) + 1

    def plane(t, carry):
        x = plane_of(t)
        for g in range((modes // MG)):
            slot = g % 2
            for j in range(nv):
                for part in range(j, MG + 1, nv):
                    if g < (modes // MG) - 1:
                        mix_part(x, g + 1, 1 - slot, part)
                    else:
                        mix_part(plane_of(t + 1), 0, 1 - slot, part)
                for h in (0, 1):
                    z = pl.ds(128 * h, 128)
                    if g == 0:
                        q = s_x = s_z = up = down = jnp.zeros((ny, 128), F32)
                    else:
                        q, s_x, s_z, up, down = (acc[i, j, :, z] for i in range(5))
                    for k in range(MG):
                        m = g * MG + k
                        here = u[m, j, x, :, z].astype(F32)
                        dx = u[m, j, x + 1, :, z].astype(F32) - u[m, j, x - 1, :, z].astype(F32)
                        dz = du_scr[slot, pl.ds(k * kv + j * ny, ny), z]
                        wx, wp, wm, wz = (w_scr[slot, k, pl.ds(i * kv + j * ny, ny), z] for i in range(4))
                        q = q + dx * wx + dz * wz
                        s_x = s_x + here * wx
                        s_z = s_z + here * wz
                        up = up + here * wm
                        down = down + here * wp
                    for i, value in enumerate((q, s_x, s_z, up, down)):
                        acc[i, j, :, z] = value
                if g == (modes // MG) - 1:
                    grad[j, x - 1] = acc[0, j] - diff_lanes(acc[2, j]) - rows_up(acc[3, j]) - rows_down(acc[4, j])
                    sx_all[j, x - 1] = acc[1, j]
        return carry

    mix_group(plane_of(0), 0, 0)
    lax.fori_loop(0, nx - 2, plane, 0)
    receive(x_links[0], has_x)
    receive(x_links[5], has_x)
    lax.fori_loop(nx - 2, nx, plane, 0)

    receive(x_links[2], has_x)
    for j in range(nv):
        field[0, j, 1] = weight[0] * (grad[j, 0] - (sx_all[j, 1] - sx[j, 0]))
        field[0, j, nx] = weight[nx - 1] * (grad[j, nx - 1] - (sx[j, 3] - sx_all[j, nx - 2]))

    def grad_plane(x, carry):
        for j in range(nv):
            field[0, j, x + 1] = weight[x] * (grad[j, x] - (sx_all[j, x + 1] - sx_all[j, x - 1]))
        return carry

    lax.fori_loop(1, nx - 1, grad_plane, 0, unroll=2)
    receive(y_links[4], has_y)
    receive(y_links[1], has_y)

    def cross(first_mode, last_mode):
        def terms(j, carry):
            for s in (0, 1):
                value = (shalo if first_mode == 0 else fterm)[s, j]
                value = -value if first_mode == 0 and s == 1 else value
                for m in range(first_mode, last_mode):
                    term = wface[s, m, pl.ds(pl.multiple_of(j * nx, nx), nx), :] * uhalo[s, m, j].astype(F32)
                    value = value - term if s == 0 else value + term
                fterm[s, j] = value
            return carry

        lax.fori_loop(0, nv, terms, 0)

    cross(0, GROUP)
    receive(y_links[5], has_y)
    cross(GROUP, modes)

    def add_rows(target, x0, weighted):
        for side in (0, 1):
            end = pl.ds((ny - 1) * side, 1)
            for x in range(nx):
                change = fterm[side, :, pl.ds(x, 1), :]
                if weighted:
                    change = change * weight[x, end, :]
                target[:, x + x0, end, :] = target[:, x + x0, end, :] + change

    add_rows(field.at[0], 1, True)

    def apply(slot):
        target = field.at[1] if slot == 0 else grad
        shift = 0 if slot == 0 else 1
        for side in (0, 1):
            for x in range(nx):
                ysend[slot, side, :, pl.ds(x, 1), :] = field[slot, :, 1 + x, pl.ds((ny - 1) * side, 1), :]
        send(y_links[2 + slot], has_y)
        send(x_links[3 + slot], has_x)

        def mixed(x, carry):
            wall[x] = dot(mat2[pl.ds(0, 4 * kv), :], split3(field[slot, :, x].reshape(kv, nz)))
            return carry

        lax.fori_loop(1, nx + 1, mixed, 0, unroll=4)
        for s in (0, 1):
            wface[s, 0] = dot(mat2[pl.ds(4 * kv, kv), :], split3(ysend[slot, s].reshape(kv, nz)))

        def result_plane(x, carry):
            for j in range(nv):
                r = pl.ds(j * ny, ny)
                wx = wall[x, r, :]
                wp, wm, wz = (wall[x, pl.ds(t * kv + j * ny, ny), :] for t in (1, 2, 3))
                here = base[j, x]
                value = base[j, x + 1] * (wx - wall[x + 1, r, :]) - base[j, x - 1] * (wx - wall[x - 1, r, :])
                value = value + base_dz[j, x - 1] * wz - diff_lanes(here * wz)
                value = value - rows_up(here * wm) - rows_down(here * wp)
                target[j, x - shift] = weight[x - 1] * value if slot == 0 else -value
            return carry

        lax.fori_loop(2, nx, result_plane, 0, unroll=2)
        if slot == 0:
            receive(x_links[1], has_x)
            receive(y_links[0], has_y)
        receive(y_links[2 + slot], has_y)
        for s in (0, 1):
            far_side = dot(mat2[pl.ds(4 * kv, kv), :], split3(yhalo[slot, s].reshape(kv, nz)))
            change = (far_side - wface[s, 0]).reshape(nv, nx, nz) * bhalo[s]
            fterm[s] = change if s == slot else -change
        receive(x_links[3 + slot], has_x)
        for x in (0, nx + 1):
            wall[x, pl.ds(0, kv), :] = dot(mat2[pl.ds(0, kv), :], split3(field[slot, :, x].reshape(kv, nz)))
        lax.fori_loop(0, 2, lambda s, carry: result_plane(1 + (nx - 1) * s, carry), 0, unroll=2)
        add_rows(target, 1 - shift, slot == 0)

    apply(0)
    apply(1)
    store = pltpu.make_async_copy(grad, out_hbm, out_sem)
    store.start()
    for link in x_links:
        drain(link, has_x)
    for link in y_links:
        drain(link, has_y)
    for copy in ones + twos + threes:
        copy.wait_send()
    store.wait()


def per_device(u, v, base, cell, pick, mix, *, interpret=False):
    modes, nv, nx, ny, nz = u.shape
    nc, nn = lax.axis_size("chord"), lax.axis_size("normal")
    kv = nv * ny
    groups = modes // GROUP
    vm = pltpu.VMEM
    any_space = pl.BlockSpec(memory_space=pl.ANY)
    smem = pl.BlockSpec(memory_space=pltpu.SMEM)
    negated = pl.pallas_call(
        functools.partial(kernel, (nc, nn, modes, nv, nx, ny, nz)),
        out_shape=jax.ShapeDtypeStruct(base.shape, F32),
        in_specs=[any_space] * 5 + [smem],
        out_specs=any_space,
        scratch_shapes=[
            vm((modes, nv, nx + 2, ny, nz), BF16),
            vm((modes, nv, nx, ny, nz), BF16),
            vm((nv, nx + 2, ny, nz), F32),
            vm((nx, ny, nz), jnp.int32),
            vm((nv, 3, nv), F32),
            vm((2, modes, nv, nx, nz), BF16),
            vm((2, modes, nv, nx, nz), BF16),
            vm((2, modes, nv, nx, nz), BF16),
            vm((2, modes, kv, nz), F32),
            vm((modes, 5 * kv, 2 * kv), BF16),
            vm((5 * kv, 3 * kv), BF16),
            vm((5 * kv, 3 * kv), F32),
            vm((2 * nx, nx * ny), BF16),
            vm((nz, nz), BF16),
            vm((2, max(GROUP, MG), 4 * kv, nz), F32),
            vm((2, MG * kv, nz), F32),
            vm((5, nv, ny, nz), F32),
            vm((nv, nx, ny, nz), F32),
            vm((nv, 4, ny, nz), F32),
            vm((nv, nx, ny, nz), F32),
            vm((2, nv, nx, nz), F32),
            vm((2, nv, nx, nz), F32),
            vm((2, 2, nv, nx, nz), F32),
            vm((2, 2, nv, nx, nz), F32),
            vm((2, nv, nx + 2, ny, nz), F32),
            vm((nx + 2, 4 * kv, nz), F32),
            vm((nv, nx, ny, nz), F32),
            vm((2, nv, nx, nz), F32),
            vm((2, nv, nx, nz), F32),
            vm((2, nv, nx, nz), F32),
            vm((3 * modes, 128), F32),
            vm((nc - 1, modes, 128), F32),
            vm((3, modes, 128), F32),
            vm((max(nn // 4 - 1, 1), modes, 128), F32),
            vm((modes, 256), F32),
            vm((nx, ny, nz), F32),
            pltpu.SemaphoreType.DMA((2 * groups + 3,)),
            pltpu.SemaphoreType.DMA((6, 2)),
            pltpu.SemaphoreType.DMA((6, 2)),
            pltpu.SemaphoreType.DMA((6, 2)),
            pltpu.SemaphoreType.DMA((6, 2)),
            pltpu.SemaphoreType.DMA((nc + nn // 4 + 1,)),
            pltpu.SemaphoreType.DMA((nc + nn // 4 + 1,)),
            pltpu.SemaphoreType.DMA,
        ],
        compiler_params=pltpu.CompilerParams(
            collective_id=0, has_side_effects=True, vmem_limit_bytes=60 * 2**20),
    )(u, v, base, cell, mix.transpose(1, 0, 2), pick)
    return -negated


def solution(mesh):
    return jax.shard_map(
        per_device,
        mesh=mesh,
        in_specs=(
            P(None, None, "chord", "normal", None),
            P(None, None, "chord", "normal", None),
            P(None, "chord", "normal", None),
            P("chord", "normal", None),
            P(),
            P(),
        ),
        out_specs=P(None, "chord", "normal", None),
        check_vma=False,
    )
```
